128 devices in a mesh: section: 8 (over x, core), ctx: 16 (over z, y).
Axes of the slice: x: 4, y: 4, z: 4, core: 2. Of those that a mesh axis runs over, the one named last changes fastest.
Arguments:
- carried_stream: float32 [8, 2048, 4096], P('section', 'ctx'), may hold values from -6 to 6
- arrival_queue: bfloat16 [2, 2048, 4096], P(None, 'ctx'), may hold values from -6 to 6
- scaling_factors: float32 [8, 4096], P('section'), may hold values from 0.25 to 1.75
- lookup_projection: bfloat16 [8, 4096, 512], P('section', 'ctx'), may hold values from -22 to 22
- content_projection: bfloat16 [8, 4096, 512], P('section', 'ctx'), may hold values from -0.1875 to 0.1875
- packed_span_lengths: int32 [10, 8], replicated, may hold values from 1 to 1024, 2048 in all within a row
- entry_permutation: int32 [2], replicated, may hold values from 0 to 1, each once
Outputs:
- produced: bfloat16 [2, 8, 2048, 4096], P(None, 'section', 'ctx')
The draws below stay inside these ranges and needn't reach their ends.
Inputs may be any that keep to these rules, and one draw needn't show every extreme that they name: `packed_span_lengths`: each row holds positive lengths summing to 2048, the largest exactly 1024. `entry_permutation`: a permutation of 0 to 1.
All inputs are finite; a program needn't handle non-finite values.
Results may differ from the reference program's by a relative error of at most 0.0082.
The reference program's roundings to bfloat16 on the way count: a program that leaves them out, or rounds other values in their place, can miss the bound.
Values may be sent and summed in bfloat16 or wider, within the bound.
No kernel may reach another device: no remote copies, remote signals or barrier semaphores. Data moves between devices by JAX's collectives and lax.ppermute only.
A program may use at most 128 MiB of HBM per device.

```python
import math
import jax
import jax.numpy as jnp
import numpy as np
from jax import lax

MODEL_WIDTH = 4096
HEAD_SIZE = 128
QUERY_HEADS = 32
KEY_VALUE_HEADS = 4
W = 2
NDOC = 8
L = 2048
SEQS = 10
N_SECTION = 8


def draw_carried_stream(key, part):
    complete_shape = (N_SECTION, L, MODEL_WIDTH)
    return jax.random.truncated_normal(jax.random.fold_in(key, 21), -12.0, 12.0, complete_shape, jnp.float32) * 0.5


def draw_lookup_projection(key, part):
    complete_shape = (N_SECTION, MODEL_WIDTH, KEY_VALUE_HEADS * HEAD_SIZE)
    drawn_part = jax.random.truncated_normal(jax.random.fold_in(key, 11), -6.0, 6.0, complete_shape, jnp.float32) * (4.0 / MODEL_WIDTH) ** 0.5
    return drawn_part.astype(jnp.bfloat16)


def level_of(key, shape, split, least, largest):
    level = 1.0
    for dim, shards_of in split:
        steps = jax.random.uniform(jax.random.fold_in(jax.random.fold_in(key, 6), dim), (shards_of,), jnp.float32, least / len(split), largest / len(split))
        level = level * jnp.repeat(jnp.exp(steps), shape[dim] // shards_of).reshape((-1,) + (1,) * (len(shape) - 1 - dim))
    return level


def split_up(number_of, total, limit, slope):
    weights = [(1 << 20) // math.isqrt(standing ** slope) + 1 for standing in range(2, number_of + 1)]
    spare, holding = total - limit - (number_of - 1), [1] * (number_of - 1)
    while spare > 0:
        candidates = [i for i in range(number_of - 1) if holding[i] < limit]
        mass, remaining = sum([weights[i] for i in candidates]), spare
        for i in candidates:
            extra = min(limit - holding[i], max(1, remaining * weights[i] // mass), spare)
            holding[i] = holding[i] + extra
            spare = spare - extra
    return np.array([limit] + holding)


def ragged_sizes(stream_key, amount, total, bound, lean):
    if amount == 2:
        one = jax.random.randint(stream_key, (), max(1, total - bound), min(bound, total - 1) + 1)
        return jnp.stack([one, total - one])
    sizes = jnp.asarray(split_up(amount, total, bound, lean), jnp.int32)
    couples = (amount - 1) // 2
    giver, taker = sizes[1:1 + 2 * couples:2], sizes[2:2 + 2 * couples:2]
    margin = jnp.minimum(giver - 1, bound - taker)
    passed = jax.random.randint(jax.random.fold_in(stream_key, 1), (couples,), 0, 1 << 20) % (margin + 1)
    sizes = sizes.at[1:1 + 2 * couples:2].set(giver - passed).at[2:2 + 2 * couples:2].set(taker + passed)
    return sizes[jax.random.permutation(jax.random.fold_in(stream_key, 2), amount)]


def gaussian(key, shape, scale, bound, cuts=(), kind=jnp.bfloat16):
    level = level_of(key, shape, cuts, -0.22, 0.18) if cuts else 1.0
    array = jax.random.normal(key, shape, jnp.float32) * scale * level
    return jnp.minimum(jnp.maximum(array, -bound), bound).astype(kind)


def setup_inputs(seed: int = 0) -> dict:
    keys = jax.random.split(jax.random.key(seed), 8)
    carried_stream = draw_carried_stream(jax.random.fold_in(keys[7], 71), 0)
    arrival_queue = gaussian(keys[1], (W, L, MODEL_WIDTH), 0.5, 6.0, ((1, 16),))
    scaling_factors = jnp.clip(1.0 + 0.15 * jax.random.normal(keys[2], (N_SECTION, MODEL_WIDTH), jnp.float32), 0.25, 1.75)
    lookup_projection = draw_lookup_projection(jax.random.fold_in(keys[7], 71), 0)
    content_projection = gaussian(keys[4], (N_SECTION, MODEL_WIDTH, KEY_VALUE_HEADS * HEAD_SIZE), (MODEL_WIDTH // 4) ** -0.5, 0.1875, ((0, 8), (1, 16)))
    packed_span_lengths = jax.vmap(lambda own: ragged_sizes(own, NDOC, L, L // 2, 2))(jax.random.split(keys[5], SEQS)).reshape((SEQS, NDOC)).astype(jnp.int32)
    entry_permutation = jax.random.permutation(keys[6], W).astype(jnp.int32)
    return dict(carried_stream=carried_stream, arrival_queue=arrival_queue, scaling_factors=scaling_factors, lookup_projection=lookup_projection, content_projection=content_projection, packed_span_lengths=packed_span_lengths, entry_permutation=entry_permutation)


EPSILON = 1e-05
MASK_FLOOR = -1e+30

def segment_ids(lengths, positions):
    ends = jnp.cumsum(lengths).astype(jnp.int32)
    return lax.optimization_barrier(jnp.sum((positions[:, None] >= ends[None, :]).astype(jnp.int32), axis=1))

def layer(skip_channel, gain, key_rows, value_rows, lengths):
    token_length = skip_channel.shape[0]
    mean_square = lax.optimization_barrier(jnp.mean(skip_channel * skip_channel, axis=-1, keepdims=True))
    normalized_input = (skip_channel * lax.rsqrt(mean_square + EPSILON) * gain).astype(jnp.bfloat16)
    gathered_keys = jnp.dot(normalized_input, key_rows, preferred_element_type=jnp.float32).astype(jnp.bfloat16)
    gathered_values = jnp.dot(normalized_input, value_rows, preferred_element_type=jnp.float32).astype(jnp.bfloat16)
    positions = jnp.arange(token_length, dtype=jnp.int32)
    segments = segment_ids(lengths, positions)
    allowed = (positions[:, None] >= positions[None, :]) & (segments[:, None] == segments[None, :])
    query_rows_set = normalized_input.reshape(token_length, KEY_VALUE_HEADS, QUERY_HEADS // KEY_VALUE_HEADS, HEAD_SIZE).transpose(1, 0, 2, 3)
    keys_by_group = gathered_keys.reshape(token_length, KEY_VALUE_HEADS, HEAD_SIZE).transpose(1, 0, 2)
    values_by_group = gathered_values.reshape(token_length, KEY_VALUE_HEADS, HEAD_SIZE).transpose(1, 0, 2)

    def one_group(operands):
        query_group, key_group, value_group = operands
        scores = jnp.einsum('tjd,sd->jts', query_group.astype(jnp.float32), key_group.astype(jnp.float32)) * HEAD_SIZE ** (-0.5)
        scores = jnp.where(allowed[None], scores, MASK_FLOOR)
        highest = lax.optimization_barrier(jnp.max(scores, axis=-1, keepdims=True))
        weights = jnp.where(allowed[None], jnp.exp(scores - highest), 0.0)
        totals = lax.optimization_barrier(jnp.sum(weights, axis=-1))
        mixed = jnp.einsum('jts,sd->tjd', weights, value_group.astype(jnp.float32), precision=lax.Precision.HIGHEST)
        return mixed / totals.T[:, :, None]
    attended = lax.map(one_group, (query_rows_set, keys_by_group, values_by_group))
    return skip_channel + attended.transpose(1, 0, 2, 3).reshape(token_length, QUERY_HEADS * HEAD_SIZE)

def apply_layer(operands):
    return layer(operands[0], operands[1], operands[2], operands[3], operands[4])

def reference(carried_stream, arrival_queue, scaling_factors, lookup_projection, content_projection, packed_span_lengths, entry_permutation):
    tier_sequence = carried_stream.shape[0]
    sequence_ids = jnp.arange(tier_sequence, dtype=jnp.int32)
    current_snapshot = carried_stream
    produced = []
    for tick in range(W):
        if tick > 0:
            chosen = entry_permutation[tick - 1].astype(jnp.int32)
            arriving = lax.dynamic_index_in_dim(arrival_queue, chosen, 0, keepdims=False).astype(jnp.float32)
            current_snapshot = jnp.concatenate([arriving[None], current_snapshot[:-1]], axis=0)
            sequence_ids = jnp.concatenate([(tier_sequence + chosen).astype(jnp.int32)[None], sequence_ids[:-1]])
        lengths = packed_span_lengths[sequence_ids]
        current_snapshot = lax.map(apply_layer, (current_snapshot, scaling_factors, lookup_projection, content_projection, lengths))
        produced.append(current_snapshot.astype(jnp.bfloat16))
    return jnp.stack(produced)
```

```python
import functools

import jax
import jax.numpy as jnp
from jax import lax
from jax.experimental import pallas as pl
from jax.experimental.pallas import tpu as pltpu
from jax.sharding import PartitionSpec as P

HEAD_SIZE = 128
QUERY_HEADS = 32
KEY_VALUE_HEADS = 4
HEAD_GROUPS = QUERY_HEADS // KEY_VALUE_HEADS
GROUP_WIDTH = HEAD_GROUPS * HEAD_SIZE
KV_WIDTH = KEY_VALUE_HEADS * HEAD_SIZE
W = 2
EPSILON = 1e-05
MASK_FLOOR = -1e30
SIDE = 4
ROWS = 2
SCALE = HEAD_SIZE ** (-0.5)
LOG2E = 1.4426950408889634


def moved(block, dz, dy):
    pairs = [
        (z * SIDE + y, ((z + dz) % SIDE) * SIDE + (y + dy) % SIDE)
        for z in range(SIDE)
        for y in range(SIDE)
    ]
    return lax.ppermute(block, "ctx", pairs)


def swapped(block, first):
    pairs = []
    for z in range(SIDE):
        for y in (first, first + 2):
            a, b = z * SIDE + y % SIDE, z * SIDE + (y + 1) % SIDE
            pairs += [(a, b), (b, a)]
    return lax.ppermute(block, "ctx", pairs)


def window_blocks(own, z, y):
    tokens = own.shape[0]
    up1 = moved(own, 1, 0)
    up2 = moved(up1, 1, 0)
    left1, right1 = moved(up1, 0, 1), moved(up1, 0, -1)
    to_right = jnp.where(y == SIDE - 1, up2, own)
    to_left = jnp.where(y == 0, own, up2)
    left2, right2 = moved(to_right, 0, 1), moved(to_left, 0, -1)
    far1 = swapped(jnp.where(y % 2 == 1, left1, right1), 1)
    far2 = swapped(jnp.where(y % 2 == 1, right2, left2), 0)
    yl, yr, yf = (y + 3) % SIDE, (y + 1) % SIDE, (y + 2) % SIDE

    def near(column):
        return jnp.where(column < y, z, z - ROWS) * SIDE + column

    order = jnp.stack(
        [
            z * SIDE + y,
            (z - 1) * SIDE + y,
            (z - 2) * SIDE + y,
            (z - 1) * SIDE + yl,
            (z - 1) * SIDE + yr,
            near(yl),
            near(yr),
            (z - 1) * SIDE + yf,
            near(yf),
        ]
    )
    return [own, up1, up2, left1, right1, left2, right2, far1, far2], order * tokens


def attention_body(n_blocks, last_tick, bases, last, q, x, starts, *refs):
    keys = refs[:n_blocks]
    values = refs[n_blocks : 2 * n_blocks]
    refs = refs[2 * n_blocks :]
    if last_tick:
        (produced,) = refs
    else:
        first, gain, produced, stream, normed, squares = refs
    g = pl.program_id(0)
    tokens = q.shape[0]
    own = bases[0]
    column = lax.broadcasted_iota(jnp.int32, (tokens, tokens), 1)
    row = lax.broadcasted_iota(jnp.int32, (tokens, tokens), 0)
    low = jnp.broadcast_to(starts[...], (tokens, tokens))
    bias = []
    for b in range(n_blocks):
        position = column + bases[b]
        allowed = (position >= low) & (position <= row + own)
        bias.append(jnp.where(allowed, 0.0, MASK_FLOOR))
    bias = jnp.concatenate(bias, axis=1)
    k = jnp.concatenate([r[...] for r in keys], axis=0)
    v = jnp.concatenate([r[...] for r in values], axis=0)
    v = jnp.concatenate([v, jnp.ones_like(v)], axis=1)
    partial = jnp.zeros((tokens, HEAD_SIZE), jnp.float32)
    for h in range(0, HEAD_GROUPS, 2):
        qs = [q[:, (h + j) * HEAD_SIZE : (h + j + 1) * HEAD_SIZE] for j in range(2)]
        s = lax.dot_general(
            jnp.concatenate(qs, axis=0),
            k,
            (((1,), (1,)), ((), ())),
            preferred_element_type=jnp.float32,
        )
        s = s + jnp.concatenate([bias, bias], axis=0)
        high = jnp.max(s, axis=1, keepdims=True)
        p = jnp.exp2((s - high) * (SCALE * LOG2E)).astype(jnp.bfloat16)
        mixed = jnp.dot(p, v, preferred_element_type=jnp.float32)
        out = mixed[:, :HEAD_SIZE] / mixed[:, HEAD_SIZE:]
        for j in range(2):
            where = slice((h + j) * HEAD_SIZE, (h + j + 1) * HEAD_SIZE)
            new = x[:, where] + out[j * tokens : (j + 1) * tokens]
            produced[:, where] = new.astype(jnp.bfloat16)
            if not last_tick:
                at = pl.ds(pl.multiple_of(g * GROUP_WIDTH, GROUP_WIDTH) + (h + j) * HEAD_SIZE, HEAD_SIZE)
                stream[:, at] = new
    if last_tick:
        return

    @pl.when(g == KEY_VALUE_HEADS - 1)
    def _():
        @pl.when(last[0] == 1)
        def _():
            stream[...] = first[...].astype(jnp.float32)

        total = jnp.zeros((tokens, 128), jnp.float32)
        for c in range(0, stream.shape[1], 128):
            piece = stream[:, c : c + 128]
            total = total + piece * piece
        mean = jnp.sum(total, axis=1, keepdims=True) * (1.0 / stream.shape[1])
        factor = lax.rsqrt(mean + EPSILON)
        for c in range(0, stream.shape[1], 128):
            at = slice(c, c + 128)
            normed[:, at] = (stream[:, at] * factor * gain[:, at]).astype(jnp.bfloat16)


def attention(blocks, bases, q, x, starts, following=None):
    tokens, width = q.shape
    n_blocks = len(blocks)
    last_tick = following is None
    flag = jnp.zeros((1,), jnp.int32) if last_tick else following[0]
    whole = lambda g, *_: (0, 0)
    by_group = pl.BlockSpec((tokens, GROUP_WIDTH), lambda g, *_: (0, g))
    in_specs = [by_group, by_group, pl.BlockSpec((tokens, 1), whole)]
    in_specs += [pl.BlockSpec((tokens, HEAD_SIZE), lambda g, *_: (0, g))] * n_blocks
    in_specs += [
        pl.BlockSpec((tokens, HEAD_SIZE), lambda g, *_: (0, KEY_VALUE_HEADS + g))
    ] * n_blocks
    out_specs = [by_group]
    out_shape = [jax.ShapeDtypeStruct((tokens, width), jnp.bfloat16)]
    operands = [q, x, starts, *blocks, *blocks]
    scratch = []
    if not last_tick:
        in_specs += [pl.BlockSpec((tokens, width), whole), pl.BlockSpec((1, width), whole)]
        operands += [following[1], following[2]]
        out_specs += [pl.BlockSpec((tokens, width), whole)] * 2
        out_shape += [
            jax.ShapeDtypeStruct((tokens, width), jnp.float32),
            jax.ShapeDtypeStruct((tokens, width), jnp.bfloat16),
        ]
        scratch = [pltpu.VMEM((8, 128), jnp.float32)]
    return pl.pallas_call(
        functools.partial(attention_body, n_blocks, last_tick),
        grid_spec=pltpu.PrefetchScalarGridSpec(
            num_scalar_prefetch=2,
            grid=(KEY_VALUE_HEADS,),
            in_specs=in_specs,
            out_specs=out_specs,
            scratch_shapes=scratch,
        ),
        out_shape=out_shape,
        compiler_params=pltpu.CompilerParams(vmem_limit_bytes=48 << 20),
        cost_estimate=pl.CostEstimate(
            flops=4 * tokens * n_blocks * tokens * width,
            transcendentals=tokens * n_blocks * tokens * QUERY_HEADS,
            bytes_accessed=tokens * width * 12 + n_blocks * tokens * 2 * KV_WIDTH * 2,
        ),
        name="attention",
    )(bases, flag, *operands)


def document_starts(lengths, positions):
    count = lengths.shape[0]
    upto = jnp.arange(count)[:, None] >= jnp.arange(count)[None, :]
    ends = jnp.sum(jnp.where(upto, lengths[None, :], 0), axis=1)
    return jnp.max(jnp.where(positions[:, None] >= ends[None, :], ends[None, :], 0), axis=1, keepdims=True)


def shards(carried, arrivals, gains, key_rows, value_rows, lengths, permutation):
    stream = carried[0]
    gain = gains[0:1]
    tokens = stream.shape[0]
    phases = lax.axis_size("section")
    phase = lax.axis_index("section")
    context = lax.axis_index("ctx")
    z, y = context // SIDE, context % SIDE
    onward = [(s, (s + 1) % phases) for s in range(phases)]
    back = [(t, s) for s, t in onward]

    weights = jnp.concatenate([key_rows[0], value_rows[0]], axis=1)
    weights = lax.all_gather(weights, "ctx", axis=0, tiled=True)

    next_gain = lax.ppermute(gain, "section", back)
    chosen = permutation[0]
    first = lax.dynamic_index_in_dim(arrivals, chosen, 0, keepdims=False)
    positions = context * tokens + jnp.arange(tokens, dtype=jnp.int32)
    sequences = [phase, jnp.where(phase == 0, phases + chosen, phase - 1)]
    starts = [
        document_starts(lax.dynamic_index_in_dim(lengths, s, 0, keepdims=False), positions)
        for s in sequences
    ]
    is_last = (phase == phases - 1).astype(jnp.int32).reshape(1)

    mean = jnp.mean(stream * stream, axis=-1, keepdims=True)
    normed = (stream * lax.rsqrt(mean + EPSILON) * gain).astype(jnp.bfloat16)
    own = jnp.dot(normed, weights, preferred_element_type=jnp.float32).astype(jnp.bfloat16)
    blocks, bases = window_blocks(own, z, y)
    early, stream, normed = attention(
        blocks, bases, normed, stream, starts[0], (is_last, first, next_gain)
    )
    normed = lax.ppermute(normed, "section", onward)
    stream = lax.ppermute(stream, "section", onward)
    own = jnp.dot(normed, weights, preferred_element_type=jnp.float32).astype(jnp.bfloat16)
    blocks, bases = window_blocks(own, z, y)
    (late,) = attention(blocks, bases, normed, stream, starts[1])
    return jnp.stack([early, late])[:, None]


def solution(mesh):
    placed = (
        P("section", "ctx", None),
        P(None, "ctx", None),
        P("section", None),
        P("section", "ctx", None),
        P("section", "ctx", None),
        P(),
        P(),
    )
    return jax.shard_map(
        shards,
        mesh=mesh,
        in_specs=placed,
        out_specs=P(None, "section", "ctx", None),
        check_vma=False,
    )
```

```python
import functools

import jax
import jax.numpy as jnp
from jax import lax
from jax.experimental import pallas as pl
from jax.experimental.pallas import tpu as pltpu
from jax.sharding import PartitionSpec as P

HEAD_SIZE = 128
QUERY_HEADS = 32
KEY_VALUE_HEADS = 4
HEAD_GROUPS = QUERY_HEADS // KEY_VALUE_HEADS
GROUP_WIDTH = HEAD_GROUPS * HEAD_SIZE
KV_WIDTH = KEY_VALUE_HEADS * HEAD_SIZE
W = 2
EPSILON = 1e-05
MASK_FLOOR = -1e30
SIDE = 4
VMEM = 56 << 20
DEPTH = 256
SCALE = HEAD_SIZE ** (-0.5)
LOG2E = 1.4426950408889634


def moved(block, dz, dy):
    pairs = [
        (z * SIDE + y, ((z + dz) % SIDE) * SIDE + (y + dy) % SIDE)
        for z in range(SIDE)
        for y in range(SIDE)
    ]
    return lax.ppermute(block, "ctx", pairs)


def swapped(block, first, along_z=False):
    pairs = []
    for other in range(SIDE):
        for at in (first, first + 2):
            a, b = at % SIDE, (at + 1) % SIDE
            if along_z:
                a, b = a * SIDE + other, b * SIDE + other
            else:
                a, b = other * SIDE + a, other * SIDE + b
            pairs += [(a, b), (b, a)]
    return lax.ppermute(block, "ctx", pairs)


def tree_gather(own, z, y):
    zp, yp, zm, ym = moved(own, 1, 0), moved(own, 0, 1), moved(own, -1, 0), moved(own, 0, -1)
    got = {(0, 0): own, (1, 0): zp, (0, 1): yp, (3, 0): zm, (0, 3): ym}
    got[0, 2] = swapped(jnp.where(y % 2 == 1, yp, ym), 1)
    got[2, 0] = swapped(jnp.where(z % 2 == 1, zm, zp), 0, True)
    got[1, 1] = moved(zp, 0, 1)
    got[3, 3] = moved(zm, 0, -1)
    got[1, 3] = moved(ym, 1, 0)
    got[3, 1] = moved(yp, -1, 0)
    got[1, 2] = moved(got[0, 2], 1, 0)
    got[3, 2] = moved(got[0, 2], -1, 0)
    got[2, 1] = moved(got[2, 0], 0, 1)
    got[2, 3] = moved(got[2, 0], 0, -1)
    got[2, 2] = moved(got[1, 2], 1, 0)
    order = [((z - dz) % SIDE) * SIDE + (y - dy) % SIDE for dz, dy in got]
    return list(got.values()), jnp.stack(order)


def window_places(y):
    yl, yr, yf = (y + 3) % SIDE, (y + 1) % SIDE, (y + 2) % SIDE
    above = [SIDE + y - c for c in (yl, yr, yf)]
    near = [jnp.where(c < y, 0, 2 * SIDE) + y - c for c in (yl, yr, yf)]
    return jnp.stack([jnp.zeros_like(y), SIDE + 0 * y, 2 * SIDE + 0 * y, *above, *near])


def window_blocks(own, y):
    up1, up2 = moved(own, 1, 0), moved(own, 2, 0)
    above = [moved(up1, 0, 1), moved(up1, 0, -1), moved(up1, 0, 2)]
    to_right = jnp.where(y == SIDE - 1, up2, own)
    to_left = jnp.where(y == 0, own, up2)
    across = jnp.where(y < 2, own, up2)
    near = [moved(to_right, 0, 1), moved(to_left, 0, -1), moved(across, 0, 2)]
    return [own, up1, up2, *above, *near]


def fetched(blocks, into, sems, first=0):
    copies, row = [], 0
    for i, block in enumerate(blocks):
        height = block.shape[0]
        copies.append(pltpu.make_async_copy(block, into.at[pl.ds(row, height)], sems.at[first + i]))
        row += height
    for copy in copies:
        copy.start()
    return copies


def by_head(out, rows, which, beside):
    if not beside:
        out[...] = rows
        return
    for h in range(KEY_VALUE_HEADS):
        at = (2 * h + which) * HEAD_SIZE
        out[:, at : at + HEAD_SIZE] = rows[:, h * HEAD_SIZE : (h + 1) * HEAD_SIZE]


def projection_body(n_keys, with_keys, with_values, order, rows, *refs):
    key_blocks, refs = refs[:n_keys], refs[n_keys:]
    if with_keys:
        keys, refs = refs[0], refs[1:]
    if with_values:
        value_rows, refs = refs[0], refs[1:]
    out, refs = refs[0], list(refs[1:])
    sems = refs.pop()
    width = rows.shape[1]
    count = width // DEPTH
    if n_keys:
        held_keys = refs.pop(0)
        key_copies = fetched(key_blocks, held_keys, sems)
    if with_values:
        held_values = refs.pop(0)
        pieces = [value_rows.at[pl.ds(j * DEPTH, DEPTH)] for j in range(count)]
        value_copies = fetched(pieces, held_values, sems, n_keys)
    if n_keys:
        total = jnp.zeros((rows.shape[0], KV_WIDTH), jnp.float32)
        for j, copy in enumerate(key_copies):
            copy.wait()
            at = pl.ds(pl.multiple_of(order[j] * DEPTH, DEPTH), DEPTH)
            part = held_keys[j * DEPTH : (j + 1) * DEPTH]
            total = total + jnp.dot(rows[:, at], part, preferred_element_type=jnp.float32)
        by_head(out, total.astype(out.dtype), 0, with_values)
    if with_keys:
        by_head(out, keys[...], 0, True)
    if with_values:
        total = jnp.zeros((rows.shape[0], KV_WIDTH), jnp.float32)
        for j, copy in enumerate(value_copies):
            copy.wait()
            at = slice(j * DEPTH, (j + 1) * DEPTH)
            total = total + jnp.dot(rows[:, at], held_values[at], preferred_element_type=jnp.float32)
        by_head(out, total.astype(out.dtype), 1, True)


def projection(rows, order, key_blocks=(), keys=None, values=None):
    tokens, width = rows.shape
    n_keys = len(key_blocks)
    in_vmem, in_hbm = pl.BlockSpec(memory_space=pltpu.VMEM), pl.BlockSpec(memory_space=pl.ANY)
    in_specs = [pl.BlockSpec(memory_space=pltpu.SMEM), in_vmem] + [in_hbm] * n_keys
    operands = [order, rows, *key_blocks]
    held = pltpu.VMEM((width, KV_WIDTH), jnp.bfloat16)
    scratch = [held] if n_keys else []
    n_copies, columns = n_keys, KV_WIDTH
    if keys is not None:
        in_specs, operands = in_specs + [in_vmem], operands + [keys]
    if values is not None:
        in_specs, operands = in_specs + [in_hbm], operands + [values]
        scratch, n_copies, columns = scratch + [held], n_copies + width // DEPTH, 2 * KV_WIDTH
    return pl.pallas_call(
        functools.partial(projection_body, n_keys, keys is not None, values is not None),
        in_specs=in_specs,
        out_specs=in_vmem,
        out_shape=jax.ShapeDtypeStruct((tokens, columns), jnp.bfloat16),
        scratch_shapes=[*scratch, pltpu.SemaphoreType.DMA((n_copies,))],
        compiler_params=pltpu.CompilerParams(vmem_limit_bytes=VMEM),
        cost_estimate=pl.CostEstimate(
            flops=2 * tokens * width * KV_WIDTH * len(scratch),
            transcendentals=0,
            bytes_accessed=len(scratch) * width * KV_WIDTH * 2,
        ),
        name="projection",
    )(*operands)


def attention_body(n_blocks, last_tick, places, last, q, x, starts, *refs):
    blocks, refs = refs[:n_blocks], refs[n_blocks:]
    if last_tick:
        _, produced = refs
    else:
        first, gain, produced, stream, normed, rows = refs
    g = pl.program_id(0)
    tokens = q.shape[0]

    column = lax.broadcasted_iota(jnp.int32, (tokens, tokens), 1)
    row = lax.broadcasted_iota(jnp.int32, (tokens, tokens), 0)
    low = jnp.broadcast_to(starts[...], (tokens, tokens))
    bias = []
    for b in range(n_blocks):
        allowed = column - places[b] * tokens >= low
        if b == 0:
            allowed = allowed & (column <= row)
        bias.append(jnp.where(allowed, 0.0, MASK_FLOOR))
    bias = jnp.concatenate(bias, axis=1)
    bias = jnp.concatenate([bias, bias], axis=0)
    k = jnp.concatenate([block[:, :HEAD_SIZE] for block in blocks], axis=0)
    v = jnp.concatenate([block[:, HEAD_SIZE:] for block in blocks], axis=0)
    v = jnp.concatenate([v, jnp.ones_like(v)], axis=1)
    for h in range(0, HEAD_GROUPS, 2):
        qs = [q[:, (h + j) * HEAD_SIZE : (h + j + 1) * HEAD_SIZE] for j in range(2)]
        s = lax.dot_general(
            jnp.concatenate(qs, axis=0),
            k,
            (((1,), (1,)), ((), ())),
            preferred_element_type=jnp.float32,
        )
        s = s + bias
        high = jnp.max(s, axis=1, keepdims=True)
        p = jnp.exp2((s - high) * (SCALE * LOG2E)).astype(jnp.bfloat16)
        mixed = jnp.dot(p, v, preferred_element_type=jnp.float32)
        out = mixed[:, :HEAD_SIZE] / mixed[:, HEAD_SIZE:]
        for j in range(2):
            where = slice((h + j) * HEAD_SIZE, (h + j + 1) * HEAD_SIZE)
            new = x[:, where] + out[j * tokens : (j + 1) * tokens]
            produced[0, :, where] = new.astype(jnp.bfloat16)
            if not last_tick:
                new = jnp.where(last[0] == 1, first[:, where].astype(jnp.float32), new)
                stream[:, where] = new
                at = pl.multiple_of(g * GROUP_WIDTH, GROUP_WIDTH) + (h + j) * HEAD_SIZE
                rows[:, pl.ds(at, HEAD_SIZE)] = new
    if last_tick:
        return

    @pl.when(g == KEY_VALUE_HEADS - 1)
    def _():
        total = jnp.zeros((tokens, 128), jnp.float32)
        for c in range(0, rows.shape[1], 128):
            piece = rows[:, c : c + 128]
            total = total + piece * piece
        mean = jnp.sum(total, axis=1, keepdims=True) * (1.0 / rows.shape[1])
        factor = lax.rsqrt(mean + EPSILON)
        for c in range(0, rows.shape[1], 128):
            at = slice(c, c + 128)
            normed[:, at] = (rows[:, at] * factor * gain[:, at]).astype(jnp.bfloat16)


def attention(blocks, places, q, x, starts, tick, onward=None, produced=None):
    tokens, width = q.shape
    n_blocks = len(blocks)
    span = sum(block.shape[0] for block in blocks)
    last_tick = onward is None
    flag = jnp.zeros((1,), jnp.int32) if last_tick else onward[0]
    whole = lambda g, *_: (0, 0)
    by_group = pl.BlockSpec((tokens, GROUP_WIDTH), lambda g, *_: (0, g))
    in_specs = [by_group, by_group, pl.BlockSpec((tokens, 1), whole)]
    in_specs += [pl.BlockSpec((tokens, 2 * HEAD_SIZE), lambda g, *_: (0, g))] * n_blocks
    out_specs = [pl.BlockSpec((1, tokens, GROUP_WIDTH), lambda g, *_: (tick, 0, g))]
    out_shape = [jax.ShapeDtypeStruct((W, tokens, width), jnp.bfloat16)]
    operands = [q, x, starts, *blocks]
    scratch = []
    aliases = {}
    if last_tick:
        aliases = {2 + len(operands): 0}
        in_specs += [pl.BlockSpec(memory_space=pl.ANY)]
        operands += [produced]
    else:
        in_specs += [by_group, pl.BlockSpec((1, width), whole)]
        operands += [onward[1], onward[2]]
        out_specs += [by_group, pl.BlockSpec((tokens, width), whole)]
        out_shape += [
            jax.ShapeDtypeStruct((tokens, width), jnp.float32),
            jax.ShapeDtypeStruct((tokens, width), jnp.bfloat16),
        ]
        scratch += [pltpu.VMEM((tokens, width), jnp.float32)]
    return pl.pallas_call(
        functools.partial(attention_body, n_blocks, last_tick),
        grid_spec=pltpu.PrefetchScalarGridSpec(
            num_scalar_prefetch=2,
            grid=(KEY_VALUE_HEADS,),
            in_specs=in_specs,
            out_specs=out_specs,
            scratch_shapes=scratch,
        ),
        out_shape=out_shape,
        input_output_aliases=aliases,
        compiler_params=pltpu.CompilerParams(vmem_limit_bytes=VMEM),
        cost_estimate=pl.CostEstimate(
            flops=4 * tokens * span * width,
            transcendentals=tokens * span * QUERY_HEADS,
            bytes_accessed=tokens * width * 12 + span * 2 * KV_WIDTH * 2,
        ),
        name="attention",
    )(places, flag, *operands)


def document_starts(lengths, positions):
    count = lengths.shape[0]
    upto = jnp.arange(count)[:, None] >= jnp.arange(count)[None, :]
    ends = jnp.sum(jnp.where(upto, lengths[None, :], 0), axis=1)
    return jnp.max(jnp.where(positions[:, None] >= ends[None, :], ends[None, :], 0), axis=1, keepdims=True)


def shards(carried, arrivals, gains, key_rows, value_rows, lengths, permutation):
    stream = carried[0]
    gain = gains[0:1]
    tokens = stream.shape[0]
    phases = lax.axis_size("section")
    phase = lax.axis_index("section")
    context = lax.axis_index("ctx")
    z, y = context // SIDE, context % SIDE
    onward = [(s, (s + 1) % phases) for s in range(phases)]
    back = [(t, s) for s, t in onward]

    value_weights = lax.all_gather(value_rows[0], "ctx", axis=0, tiled=True)
    key_blocks, order = tree_gather(key_rows[0], z, y)

    next_gain = lax.ppermute(gain, "section", back)
    chosen = permutation[0]
    first = lax.dynamic_index_in_dim(arrivals, chosen, 0, keepdims=False)
    positions = context * tokens + jnp.arange(tokens, dtype=jnp.int32)
    sequences = [phase, jnp.where(phase == 0, phases + chosen, phase - 1)]
    starts = [
        document_starts(lax.dynamic_index_in_dim(lengths, s, 0, keepdims=False), positions) - context * tokens
        for s in sequences
    ]
    is_last = (phase == phases - 1).astype(jnp.int32).reshape(1)

    mean = jnp.mean(stream * stream, axis=-1, keepdims=True)
    normed = (stream * lax.rsqrt(mean + EPSILON) * gain).astype(jnp.bfloat16)
    places = window_places(y)
    keys = projection(normed, order, key_blocks)
    own = projection(normed, order, (), keys, value_weights)
    blocks = window_blocks(own, y)
    produced, stream, normed = attention(
        blocks, places, normed, stream, starts[0], 0, (is_last, first, next_gain)
    )
    normed = lax.ppermute(normed, "section", onward)
    normed, stream = lax.optimization_barrier((normed, stream))
    stream = lax.ppermute(stream, "section", onward)
    own = projection(normed, order, key_blocks, None, value_weights)
    blocks = window_blocks(own, y)
    (produced,) = attention(blocks, places, normed, stream, starts[1], 1, None, produced)
    return produced[:, None]


def solution(mesh):
    placed = (
        P("section", "ctx", None),
        P(None, "ctx", None),
        P("section", None),
        P("section", "ctx", None),
        P("section", "ctx", None),
        P(),
        P(),
    )
    return jax.shard_map(
        shards,
        mesh=mesh,
        in_specs=placed,
        out_specs=P(None, "section", "ctx", None),
        check_vma=False,
    )
```

```python
import functools

import jax
import jax.numpy as jnp
from jax import lax
from jax.experimental import pallas as pl
from jax.experimental.pallas import tpu as pltpu
from jax.sharding import PartitionSpec as P

HEAD_SIZE = 128
QUERY_HEADS = 32
KEY_VALUE_HEADS = 4
HEAD_GROUPS = QUERY_HEADS // KEY_VALUE_HEADS
GROUP_WIDTH = HEAD_GROUPS * HEAD_SIZE
KV_WIDTH = KEY_VALUE_HEADS * HEAD_SIZE
W = 2
EPSILON = 1e-05
MASK_FLOOR = -1e30
SIDE = 4
VMEM = 28 << 20
TOGETHER = 4
DEPTH = 256
SCALE = HEAD_SIZE ** (-0.5)
LOG2E = 1.4426950408889634


def moved(block, dz, dy):
    pairs = [
        (z * SIDE + y, ((z + dz) % SIDE) * SIDE + (y + dy) % SIDE)
        for z in range(SIDE)
        for y in range(SIDE)
    ]
    return lax.ppermute(block, "ctx", pairs)


def swapped(block, first, along_z=False):
    pairs = []
    for other in range(SIDE):
        for at in (first, first + 2):
            a, b = at % SIDE, (at + 1) % SIDE
            if along_z:
                a, b = a * SIDE + other, b * SIDE + other
            else:
                a, b = other * SIDE + a, other * SIDE + b
            pairs += [(a, b), (b, a)]
    return lax.ppermute(block, "ctx", pairs)


def tree_gather(own, z, y):
    zp, yp, zm, ym = moved(own, 1, 0), moved(own, 0, 1), moved(own, -1, 0), moved(own, 0, -1)
    got = {(0, 0): own, (1, 0): zp, (0, 1): yp, (3, 0): zm, (0, 3): ym}
    got[0, 2] = swapped(jnp.where(y % 2 == 1, yp, ym), 1)
    got[2, 0] = swapped(jnp.where(z % 2 == 1, zm, zp), 0, True)
    got[1, 1] = moved(zp, 0, 1)
    got[3, 3] = moved(zm, 0, -1)
    got[1, 3] = moved(ym, 1, 0)
    got[3, 1] = moved(yp, -1, 0)
    got[1, 2] = moved(got[0, 2], 1, 0)
    got[3, 2] = moved(got[0, 2], -1, 0)
    got[2, 1] = moved(got[2, 0], 0, 1)
    got[2, 3] = moved(got[2, 0], 0, -1)
    got[2, 2] = moved(got[1, 2], 1, 0)
    order = [((z - dz) % SIDE) * SIDE + (y - dy) % SIDE for dz, dy in got]
    return list(got.values()), jnp.stack(order)


def window_places(y):
    yl, yr, yf = (y + 3) % SIDE, (y + 1) % SIDE, (y + 2) % SIDE
    above = [SIDE + y - c for c in (yl, yr, yf)]
    near = [jnp.where(c < y, 0, 2 * SIDE) + y - c for c in (yl, yr, yf)]
    return jnp.stack([jnp.zeros_like(y), SIDE + 0 * y, 2 * SIDE + 0 * y, *above, *near])


def window_blocks(own, y):
    up1 = moved(own, 1, 0)
    up2 = moved(up1, 1, 0)
    above = [moved(up1, 0, 1), moved(up1, 0, -1), moved(up1, 0, 2)]
    to_right = jnp.where(y == SIDE - 1, up2, own)
    to_left = jnp.where(y == 0, own, up2)
    across = jnp.where(y < 2, own, up2)
    near = [moved(to_right, 0, 1), moved(to_left, 0, -1), moved(across, 0, 2)]
    return [own, up1, up2, *above], near


def fetched(blocks, into, sems, first=0):
    copies, row = [], 0
    for i, block in enumerate(blocks):
        height = block.shape[0]
        copies.append(pltpu.make_async_copy(block, into.at[pl.ds(row, height)], sems.at[first + i]))
        row += height
    for copy in copies:
        copy.start()
    return copies


def by_head(out, rows, which, beside):
    if not beside:
        out[...] = rows
        return
    for h in range(KEY_VALUE_HEADS):
        at = (2 * h + which) * HEAD_SIZE
        out[:, at : at + HEAD_SIZE] = rows[:, h * HEAD_SIZE : (h + 1) * HEAD_SIZE]


def projection_body(n_keys, with_keys, with_values, order, rows, *refs):
    key_blocks, refs = refs[:n_keys], refs[n_keys:]
    if with_keys:
        keys, refs = refs[0], refs[1:]
    if with_values:
        value_rows, refs = refs[0], refs[1:]
    out, refs = refs[0], list(refs[1:])
    sems = refs.pop()
    width = rows.shape[1]
    count = width // DEPTH
    if n_keys:
        held_keys = refs.pop(0)
        key_copies = fetched(key_blocks, held_keys, sems)
    if with_values:
        held_values = refs.pop(0)
        pieces = [value_rows.at[pl.ds(j * DEPTH, DEPTH)] for j in range(count)]
        value_copies = fetched(pieces, held_values, sems, n_keys)
    if n_keys:
        total = jnp.zeros((rows.shape[0], KV_WIDTH), jnp.float32)
        for j, copy in enumerate(key_copies):
            copy.wait()
            at = pl.ds(pl.multiple_of(order[j] * DEPTH, DEPTH), DEPTH)
            part = held_keys[j * DEPTH : (j + 1) * DEPTH]
            total = total + jnp.dot(rows[:, at], part, preferred_element_type=jnp.float32)
        by_head(out, total.astype(out.dtype), 0, with_values)
    if with_keys:
        by_head(out, keys[...], 0, True)
    if with_values:
        total = jnp.zeros((rows.shape[0], KV_WIDTH), jnp.float32)
        for j, copy in enumerate(value_copies):
            copy.wait()
            at = slice(j * DEPTH, (j + 1) * DEPTH)
            total = total + jnp.dot(rows[:, at], held_values[at], preferred_element_type=jnp.float32)
        by_head(out, total.astype(out.dtype), 1, True)


def projection(rows, order, key_blocks=(), keys=None, values=None):
    tokens, width = rows.shape
    n_keys = len(key_blocks)
    in_vmem, in_hbm = pl.BlockSpec(memory_space=pltpu.VMEM), pl.BlockSpec(memory_space=pl.ANY)
    in_specs = [pl.BlockSpec(memory_space=pltpu.SMEM), in_vmem] + [in_hbm] * n_keys
    operands = [order, rows, *key_blocks]
    held = pltpu.VMEM((width, KV_WIDTH), jnp.bfloat16)
    scratch = [held] if n_keys else []
    n_copies, columns = n_keys, KV_WIDTH
    if keys is not None:
        in_specs, operands = in_specs + [in_vmem], operands + [keys]
    if values is not None:
        in_specs, operands = in_specs + [in_hbm], operands + [values]
        scratch, n_copies, columns = scratch + [held], n_copies + width // DEPTH, 2 * KV_WIDTH
    return pl.pallas_call(
        functools.partial(projection_body, n_keys, keys is not None, values is not None),
        in_specs=in_specs,
        out_specs=in_vmem,
        out_shape=jax.ShapeDtypeStruct((tokens, columns), jnp.bfloat16),
        scratch_shapes=[*scratch, pltpu.SemaphoreType.DMA((n_copies,))],
        compiler_params=pltpu.CompilerParams(vmem_limit_bytes=VMEM),
        cost_estimate=pl.CostEstimate(
            flops=2 * tokens * width * KV_WIDTH * len(scratch),
            transcendentals=0,
            bytes_accessed=len(scratch) * width * KV_WIDTH * 2,
        ),
        name="projection",
    )(*operands)


def attention_body(n_blocks, stage, places, last, q, starts, *refs):
    blocks, refs = refs[:n_blocks], refs[n_blocks:]
    if stage == "first":
        out_mix, out_sum, out_high = refs
    elif stage == "last":
        x, mix, sums, highs, _, produced = refs
    else:
        x, mix, sums, highs, first, gain, produced, stream, normed, rows = refs
    g = pl.program_id(0)
    tokens = q.shape[0]
    column = lax.broadcasted_iota(jnp.int32, (tokens, tokens), 1)
    row = lax.broadcasted_iota(jnp.int32, (tokens, tokens), 0)
    low = jnp.broadcast_to(starts[...], (tokens, tokens))
    bias = []
    for b in range(n_blocks):
        allowed = column - places[b] * tokens >= low
        if stage == "first" and b == 0:
            allowed = allowed & (column <= row)
        bias.append(jnp.where(allowed, 0.0, MASK_FLOOR))
    bias = jnp.concatenate(bias, axis=1)
    bias = jnp.concatenate([bias] * TOGETHER, axis=0)
    k = jnp.concatenate([block[:, :HEAD_SIZE] for block in blocks], axis=0)
    v = jnp.concatenate([block[:, HEAD_SIZE:] for block in blocks], axis=0)
    v = jnp.concatenate([v, jnp.ones_like(v)], axis=1)
    for h in range(0, HEAD_GROUPS, TOGETHER):
        qs = [q[:, (h + j) * HEAD_SIZE : (h + j + 1) * HEAD_SIZE] for j in range(TOGETHER)]
        s = lax.dot_general(
            jnp.concatenate(qs, axis=0),
            k,
            (((1,), (1,)), ((), ())),
            preferred_element_type=jnp.float32,
        )
        s = s + bias
        here = slice(h * tokens, (h + TOGETHER) * tokens)
        high = jnp.max(s, axis=1, keepdims=True)
        high = jnp.broadcast_to(high, (high.shape[0], HEAD_SIZE))
        if stage != "first":
            before = highs[here]
            high = jnp.maximum(high, before)
        p = jnp.concatenate(
            [
                jnp.exp2((s[:, c : c + HEAD_SIZE] - high) * (SCALE * LOG2E))
                for c in range(0, s.shape[1], HEAD_SIZE)
            ],
            axis=1,
        ).astype(jnp.bfloat16)
        mixed = jnp.dot(p, v, preferred_element_type=jnp.float32)
        mixed, total = mixed[:, :HEAD_SIZE], mixed[:, HEAD_SIZE:]
        if stage == "first":
            out_mix[here], out_sum[here], out_high[here] = mixed, total, high
            continue
        kept = jnp.exp2((before - high) * (SCALE * LOG2E))
        out = (mixed + mix[here] * kept) / (total + sums[here] * kept)
        for j in range(TOGETHER):
            where = slice((h + j) * HEAD_SIZE, (h + j + 1) * HEAD_SIZE)
            new = x[:, where] + out[j * tokens : (j + 1) * tokens]
            produced[0, :, where] = new.astype(jnp.bfloat16)
            if stage != "last":
                new = jnp.where(last[0] == 1, first[:, where].astype(jnp.float32), new)
                stream[:, where] = new
                at = pl.multiple_of(g * GROUP_WIDTH, GROUP_WIDTH) + (h + j) * HEAD_SIZE
                rows[:, pl.ds(at, HEAD_SIZE)] = new
    if stage != "onward":
        return

    @pl.when(g == KEY_VALUE_HEADS - 1)
    def _():
        total = jnp.zeros((tokens, 128), jnp.float32)
        for c in range(0, rows.shape[1], 128):
            piece = rows[:, c : c + 128]
            total = total + piece * piece
        mean = jnp.sum(total, axis=1, keepdims=True) * (1.0 / rows.shape[1])
        factor = lax.rsqrt(mean + EPSILON)
        for c in range(0, rows.shape[1], 128):
            at = slice(c, c + 128)
            normed[:, at] = (rows[:, at] * factor * gain[:, at]).astype(jnp.bfloat16)


def attention(blocks, places, q, starts, part=None, x=None, onward=None, produced=None):
    tokens, width = q.shape
    n_blocks = len(blocks)
    span = n_blocks * tokens
    stage = "first" if part is None else "last" if onward is None else "onward"
    flag = jnp.zeros((1,), jnp.int32) if onward is None else onward[0]
    whole = lambda g, *_: (0, 0)
    by_group = pl.BlockSpec((tokens, GROUP_WIDTH), lambda g, *_: (0, g))
    by_rows = pl.BlockSpec((HEAD_GROUPS * tokens, HEAD_SIZE), lambda g, *_: (g, 0))
    in_specs = [by_group, pl.BlockSpec((tokens, 1), whole)]
    in_specs += [pl.BlockSpec((tokens, 2 * HEAD_SIZE), lambda g, *_: (0, g))] * n_blocks
    operands = [q, starts, *blocks]
    scratch = []
    aliases = {}
    if stage == "first":
        out_specs = [by_rows] * 3
        out_shape = [jax.ShapeDtypeStruct((QUERY_HEADS * tokens, HEAD_SIZE), jnp.float32)] * 3
    else:
        tick = 0 if stage == "onward" else W - 1
        in_specs += [by_group] + [by_rows] * 3
        operands += [x, *part]
        out_specs = [pl.BlockSpec((1, tokens, GROUP_WIDTH), lambda g, *_: (tick, 0, g))]
        out_shape = [jax.ShapeDtypeStruct((W, tokens, width), jnp.bfloat16)]
    if stage == "last":
        aliases = {2 + len(operands): 0}
        in_specs += [pl.BlockSpec(memory_space=pl.ANY)]
        operands += [produced]
    if stage == "onward":
        in_specs += [by_group, pl.BlockSpec((1, width), whole)]
        operands += [onward[1], onward[2]]
        out_specs += [by_group, pl.BlockSpec((tokens, width), whole)]
        out_shape += [
            jax.ShapeDtypeStruct((tokens, width), jnp.float32),
            jax.ShapeDtypeStruct((tokens, width), jnp.bfloat16),
        ]
        scratch += [pltpu.VMEM((tokens, width), jnp.float32)]
    return pl.pallas_call(
        functools.partial(attention_body, n_blocks, stage),
        grid_spec=pltpu.PrefetchScalarGridSpec(
            num_scalar_prefetch=2,
            grid=(KEY_VALUE_HEADS,),
            in_specs=in_specs,
            out_specs=out_specs,
            scratch_shapes=scratch,
        ),
        out_shape=out_shape,
        input_output_aliases=aliases,
        compiler_params=pltpu.CompilerParams(vmem_limit_bytes=VMEM),
        cost_estimate=pl.CostEstimate(
            flops=4 * tokens * span * width,
            transcendentals=tokens * span * QUERY_HEADS,
            bytes_accessed=tokens * width * 12 + span * 2 * KV_WIDTH * 2,
        ),
        name="attention",
    )(places, flag, *operands)


def document_starts(lengths, positions):
    count = lengths.shape[0]
    upto = jnp.arange(count)[:, None] >= jnp.arange(count)[None, :]
    ends = jnp.sum(jnp.where(upto, lengths[None, :], 0), axis=1)
    return jnp.max(jnp.where(positions[:, None] >= ends[None, :], ends[None, :], 0), axis=1, keepdims=True)


def shards(carried, arrivals, gains, key_rows, value_rows, lengths, permutation):
    stream = carried[0]
    gain = gains[0:1]
    tokens = stream.shape[0]
    phases = lax.axis_size("section")
    phase = lax.axis_index("section")
    context = lax.axis_index("ctx")
    z, y = context // SIDE, context % SIDE
    onward = [(s, (s + 1) % phases) for s in range(phases)]
    back = [(t, s) for s, t in onward]

    value_weights = lax.all_gather(value_rows[0], "ctx", axis=0, tiled=True)
    key_blocks, order = tree_gather(key_rows[0], z, y)

    next_gain = lax.ppermute(gain, "section", back)
    chosen = permutation[0]
    first = lax.dynamic_index_in_dim(arrivals, chosen, 0, keepdims=False)
    positions = context * tokens + jnp.arange(tokens, dtype=jnp.int32)
    sequences = [phase, jnp.where(phase == 0, phases + chosen, phase - 1)]
    starts = [
        document_starts(lax.dynamic_index_in_dim(lengths, s, 0, keepdims=False), positions) - context * tokens
        for s in sequences
    ]
    is_last = (phase == phases - 1).astype(jnp.int32).reshape(1)

    mean = jnp.mean(stream * stream, axis=-1, keepdims=True)
    normed = (stream * lax.rsqrt(mean + EPSILON) * gain).astype(jnp.bfloat16)
    places = window_places(y)
    keys = projection(normed, order, key_blocks)
    own = projection(normed, order, (), keys, value_weights)
    early, late = window_blocks(own, y)
    part = attention(early, places[: len(early)], normed, starts[0])
    produced, stream, normed = attention(
        late, places[len(early) :], normed, starts[0], part, stream, (is_last, first, next_gain)
    )
    normed = lax.ppermute(normed, "section", onward)
    normed, stream = lax.optimization_barrier((normed, stream))
    stream = lax.ppermute(stream, "section", onward)
    own = projection(normed, order, key_blocks, None, value_weights)
    early, late = window_blocks(own, y)
    part = attention(early, places[: len(early)], normed, starts[1])
    (produced,) = attention(late, places[len(early) :], normed, starts[1], part, stream, None, produced)
    return produced[:, None]


def solution(mesh):
    placed = (
        P("section", "ctx", None),
        P(None, "ctx", None),
        P("section", None),
        P("section", "ctx", None),
        P("section", "ctx", None),
        P(),
        P(),
    )
    return jax.shard_map(
        shards,
        mesh=mesh,
        in_specs=placed,
        out_specs=P(None, "section", "ctx", None),
        check_vma=False,
    )
```

```python
import functools

import jax
import jax.numpy as jnp
from jax import lax
from jax.experimental import pallas as pl
from jax.experimental.pallas import tpu as pltpu
from jax.sharding import PartitionSpec as P

HEAD_SIZE = 128
QUERY_HEADS = 32
KEY_VALUE_HEADS = 4
HEAD_GROUPS = QUERY_HEADS // KEY_VALUE_HEADS
GROUP_WIDTH = HEAD_GROUPS * HEAD_SIZE
KV_WIDTH = KEY_VALUE_HEADS * HEAD_SIZE
W = 2
EPSILON = 1e-05
MASK_FLOOR = -1e30
SIDE = 4
VMEM = 28 << 20
WHOLE = 56 << 20
DOCUMENTS = 8
PLACES = 9
INFO = PLACES + W * (1 + DOCUMENTS) + 1
TOGETHER = 4
DEPTH = 256
SCALE = HEAD_SIZE ** (-0.5)
LOG2E = 1.4426950408889634


def moved(block, dz, dy):
    pairs = [
        (z * SIDE + y, ((z + dz) % SIDE) * SIDE + (y + dy) % SIDE)
        for z in range(SIDE)
        for y in range(SIDE)
    ]
    return lax.ppermute(block, "ctx", pairs)


def tree_gather(own, z, y):
    zp, yp, zm, ym = moved(own, 1, 0), moved(own, 0, 1), moved(own, -1, 0), moved(own, 0, -1)
    got = {(0, 0): own, (1, 0): zp, (0, 1): yp, (3, 0): zm, (0, 3): ym}
    got[0, 2], got[2, 0] = moved(own, 0, 2), moved(own, 2, 0)
    got[1, 1] = moved(zp, 0, 1)
    got[3, 3] = moved(zm, 0, -1)
    got[1, 3] = moved(ym, 1, 0)
    got[3, 1] = moved(yp, -1, 0)
    got[1, 2] = moved(got[0, 2], 1, 0)
    got[3, 2] = moved(got[0, 2], -1, 0)
    got[2, 1] = moved(got[2, 0], 0, 1)
    got[2, 3] = moved(got[2, 0], 0, -1)
    got[2, 2] = moved(got[1, 2], 1, 0)
    order = [((z - dz) % SIDE) * SIDE + (y - dy) % SIDE for dz, dy in got]
    return list(got.values()), jnp.stack(order)


def window_places(y):
    yl, yr, yf = (y + 3) % SIDE, (y + 1) % SIDE, (y + 2) % SIDE
    above = [SIDE + y - c for c in (yl, yr, yf)]
    near = [jnp.where(c < y, 0, 2 * SIDE) + y - c for c in (yl, yr, yf)]
    return jnp.stack([jnp.zeros_like(y), SIDE + 0 * y, 2 * SIDE + 0 * y, *above, *near])


def window_blocks(own, y):
    up1 = moved(own, 1, 0)
    up2 = moved(up1, 1, 0)
    above = [moved(up1, 0, 1), moved(up1, 0, -1), moved(up1, 0, 2)]
    to_right = jnp.where(y == SIDE - 1, up2, own)
    to_left = jnp.where(y == 0, own, up2)
    across = jnp.where(y < 2, own, up2)
    near = [moved(to_right, 0, 1), moved(to_left, 0, -1), moved(across, 0, 2)]
    return [own, up1, up2, *above], near


def fetched(blocks, into, sems, first=0):
    copies, row = [], 0
    for i, block in enumerate(blocks):
        height = block.shape[0]
        copies.append(pltpu.make_async_copy(block, into.at[pl.ds(row, height)], sems.at[first + i]))
        row += height
    for copy in copies:
        copy.start()
    return copies


def by_head(out, rows, which, beside):
    if not beside:
        out[...] = rows
        return
    for h in range(KEY_VALUE_HEADS):
        at = (2 * h + which) * HEAD_SIZE
        out[:, at : at + HEAD_SIZE] = rows[:, h * HEAD_SIZE : (h + 1) * HEAD_SIZE]


def projection_body(n_keys, with_keys, with_values, order, rows, *refs):
    key_blocks, refs = refs[:n_keys], refs[n_keys:]
    if with_keys:
        keys, refs = refs[0], refs[1:]
    if with_values:
        value_rows, refs = refs[0], refs[1:]
    out, refs = refs[0], list(refs[1:])
    sems = refs.pop()
    width = rows.shape[1]
    count = width // DEPTH
    if n_keys:
        held_keys = refs.pop(0)
        key_copies = fetched(key_blocks, held_keys, sems)
    if with_values:
        held_values = refs.pop(0)
        pieces = [value_rows.at[pl.ds(j * DEPTH, DEPTH)] for j in range(count)]
        value_copies = fetched(pieces, held_values, sems, n_keys)
    if n_keys:
        total = jnp.zeros((rows.shape[0], KV_WIDTH), jnp.float32)
        for j, copy in enumerate(key_copies):
            copy.wait()
            at = pl.ds(pl.multiple_of(order[j] * DEPTH, DEPTH), DEPTH)
            part = held_keys[j * DEPTH : (j + 1) * DEPTH]
            total = total + jnp.dot(rows[:, at], part, preferred_element_type=jnp.float32)
        by_head(out, total.astype(out.dtype), 0, with_values)
    if with_keys:
        by_head(out, keys[...], 0, True)
    if with_values:
        total = jnp.zeros((rows.shape[0], KV_WIDTH), jnp.float32)
        for j, copy in enumerate(value_copies):
            copy.wait()
            at = slice(j * DEPTH, (j + 1) * DEPTH)
            total = total + jnp.dot(rows[:, at], held_values[at], preferred_element_type=jnp.float32)
        by_head(out, total.astype(out.dtype), 1, True)


def projection(rows, order, key_blocks=(), keys=None, values=None, vmem=VMEM):
    tokens, width = rows.shape
    n_keys = len(key_blocks)
    in_vmem, in_hbm = pl.BlockSpec(memory_space=pltpu.VMEM), pl.BlockSpec(memory_space=pl.ANY)
    in_specs = [pl.BlockSpec(memory_space=pltpu.SMEM), in_vmem] + [in_hbm] * n_keys
    operands = [order, rows, *key_blocks]
    held = pltpu.VMEM((width, KV_WIDTH), jnp.bfloat16)
    scratch = [held] if n_keys else []
    n_copies, columns = n_keys, KV_WIDTH
    if keys is not None:
        in_specs, operands = in_specs + [in_vmem], operands + [keys]
    if values is not None:
        in_specs, operands = in_specs + [in_hbm], operands + [values]
        scratch, n_copies, columns = scratch + [held], n_copies + width // DEPTH, 2 * KV_WIDTH
    return pl.pallas_call(
        functools.partial(projection_body, n_keys, keys is not None, values is not None),
        in_specs=in_specs,
        out_specs=in_vmem,
        out_shape=jax.ShapeDtypeStruct((tokens, columns), jnp.bfloat16),
        scratch_shapes=[*scratch, pltpu.SemaphoreType.DMA((n_copies,))],
        compiler_params=pltpu.CompilerParams(vmem_limit_bytes=vmem),
        cost_estimate=pl.CostEstimate(
            flops=2 * tokens * width * KV_WIDTH * len(scratch),
            transcendentals=0,
            bytes_accessed=len(scratch) * width * KV_WIDTH * 2,
        ),
        name="projection",
    )(*operands)


def attention_body(n_blocks, stage, tick, info, q, *refs):
    blocks, refs = refs[:n_blocks], refs[n_blocks:]
    if stage == "first":
        out_mix, out_sum, out_high = refs
    elif stage == "last":
        x, mix, sums, highs, _, produced = refs
    else:
        x, mix, sums, highs, first, gain, produced, stream, normed, rows = refs
    g = pl.program_id(0)
    tokens = q.shape[0]
    column = lax.broadcasted_iota(jnp.int32, (tokens, tokens), 1)
    row = lax.broadcasted_iota(jnp.int32, (tokens, tokens), 0)
    ends = PLACES + tick * (1 + DOCUMENTS)
    low = jnp.full((tokens, tokens), info[ends], jnp.int32)
    for j in range(1, 1 + DOCUMENTS):
        low = jnp.where(row >= info[ends + j], info[ends + j], low)
    bias = []
    for b in range(n_blocks):
        place = info[b if stage == "first" else PLACES - n_blocks + b]
        allowed = column - place * tokens >= low
        if stage == "first" and b == 0:
            allowed = allowed & (column <= row)
        bias.append(jnp.where(allowed, 0.0, MASK_FLOOR))
    bias = jnp.concatenate(bias, axis=1)
    bias = jnp.concatenate([bias] * TOGETHER, axis=0)
    k = jnp.concatenate([block[:, :HEAD_SIZE] for block in blocks], axis=0)
    v = jnp.concatenate([block[:, HEAD_SIZE:] for block in blocks], axis=0)
    v = jnp.concatenate([v, jnp.ones_like(v)], axis=1)
    for h in range(0, HEAD_GROUPS, TOGETHER):
        qs = [q[:, (h + j) * HEAD_SIZE : (h + j + 1) * HEAD_SIZE] for j in range(TOGETHER)]
        s = lax.dot_general(
            jnp.concatenate(qs, axis=0),
            k,
            (((1,), (1,)), ((), ())),
            preferred_element_type=jnp.float32,
        )
        s = s + bias
        here = slice(h * tokens, (h + TOGETHER) * tokens)
        high = jnp.max(s, axis=1, keepdims=True)
        high = jnp.broadcast_to(high, (high.shape[0], HEAD_SIZE))
        if stage != "first":
            before = highs[here]
            high = jnp.maximum(high, before)
        p = jnp.concatenate(
            [
                jnp.exp2((s[:, c : c + HEAD_SIZE] - high) * (SCALE * LOG2E))
                for c in range(0, s.shape[1], HEAD_SIZE)
            ],
            axis=1,
        ).astype(jnp.bfloat16)
        mixed = jnp.dot(p, v, preferred_element_type=jnp.float32)
        mixed, total = mixed[:, :HEAD_SIZE], mixed[:, HEAD_SIZE:]
        if stage == "first":
            out_mix[here], out_sum[here], out_high[here] = mixed, total, high
            continue
        kept = jnp.exp2((before - high) * (SCALE * LOG2E))
        out = (mixed + mix[here] * kept) / (total + sums[here] * kept)
        for j in range(TOGETHER):
            where = slice((h + j) * HEAD_SIZE, (h + j + 1) * HEAD_SIZE)
            new = x[:, where] + out[j * tokens : (j + 1) * tokens]
            produced[0, :, where] = new.astype(jnp.bfloat16)
            if stage != "last":
                new = jnp.where(info[INFO - 1] == 1, first[:, where].astype(jnp.float32), new)
                stream[:, where] = new
                at = pl.multiple_of(g * GROUP_WIDTH, GROUP_WIDTH) + (h + j) * HEAD_SIZE
                rows[:, pl.ds(at, HEAD_SIZE)] = new
    if stage != "onward":
        return

    @pl.when(g == KEY_VALUE_HEADS - 1)
    def _():
        total = jnp.zeros((tokens, 128), jnp.float32)
        for c in range(0, rows.shape[1], 128):
            piece = rows[:, c : c + 128]
            total = total + piece * piece
        mean = jnp.sum(total, axis=1, keepdims=True) * (1.0 / rows.shape[1])
        factor = lax.rsqrt(mean + EPSILON)
        for c in range(0, rows.shape[1], 128):
            at = slice(c, c + 128)
            normed[:, at] = (rows[:, at] * factor * gain[:, at]).astype(jnp.bfloat16)


def attention(blocks, info, tick, q, part=None, x=None, onward=None, produced=None):
    tokens, width = q.shape
    n_blocks = len(blocks)
    span = n_blocks * tokens
    stage = "first" if part is None else "last" if onward is None else "onward"
    whole = lambda g, *_: (0, 0)
    by_group = pl.BlockSpec((tokens, GROUP_WIDTH), lambda g, *_: (0, g))
    by_rows = pl.BlockSpec((HEAD_GROUPS * tokens, HEAD_SIZE), lambda g, *_: (g, 0))
    in_specs = [by_group]
    in_specs += [pl.BlockSpec((tokens, 2 * HEAD_SIZE), lambda g, *_: (0, g))] * n_blocks
    operands = [q, *blocks]
    scratch = []
    aliases = {}
    if stage == "first":
        out_specs = [by_rows] * 3
        out_shape = [jax.ShapeDtypeStruct((QUERY_HEADS * tokens, HEAD_SIZE), jnp.float32)] * 3
    else:
        in_specs += [by_group] + [by_rows] * 3
        operands += [x, *part]
        out_specs = [pl.BlockSpec((1, tokens, GROUP_WIDTH), lambda g, *_: (tick, 0, g))]
        out_shape = [jax.ShapeDtypeStruct((W, tokens, width), jnp.bfloat16)]
    if stage == "last":
        aliases = {1 + len(operands): 0}
        in_specs += [pl.BlockSpec(memory_space=pl.ANY)]
        operands += [produced]
    if stage == "onward":
        in_specs += [by_group, pl.BlockSpec((1, width), whole)]
        operands += [*onward]
        out_specs += [by_group, pl.BlockSpec((tokens, width), whole)]
        out_shape += [
            jax.ShapeDtypeStruct((tokens, width), jnp.float32),
            jax.ShapeDtypeStruct((tokens, width), jnp.bfloat16),
        ]
        scratch += [pltpu.VMEM((tokens, width), jnp.float32)]
    return pl.pallas_call(
        functools.partial(attention_body, n_blocks, stage, tick),
        grid_spec=pltpu.PrefetchScalarGridSpec(
            num_scalar_prefetch=1,
            grid=(KEY_VALUE_HEADS,),
            in_specs=in_specs,
            out_specs=out_specs,
            scratch_shapes=scratch,
        ),
        out_shape=out_shape,
        input_output_aliases=aliases,
        compiler_params=pltpu.CompilerParams(vmem_limit_bytes=VMEM),
        cost_estimate=pl.CostEstimate(
            flops=4 * tokens * span * width,
            transcendentals=tokens * span * QUERY_HEADS,
            bytes_accessed=tokens * width * 12 + span * 2 * KV_WIDTH * 2,
        ),
        name="attention",
    )(info, *operands)


def document_bounds(lengths, own_first):
    count = lengths.shape[0]
    upto = jnp.arange(count + 1)[:, None] > jnp.arange(count)[None, :]
    return jnp.sum(jnp.where(upto, lengths[None, :], 0), axis=1) - own_first


def shards(carried, arrivals, gains, key_rows, value_rows, lengths, permutation):
    stream = carried[0]
    gain = gains[0:1]
    tokens = stream.shape[0]
    phases = lax.axis_size("section")
    phase = lax.axis_index("section")
    context = lax.axis_index("ctx")
    z, y = context // SIDE, context % SIDE
    onward = [(s, (s + 1) % phases) for s in range(phases)]
    back = [(t, s) for s, t in onward]

    value_weights = lax.all_gather(value_rows[0], "ctx", axis=0, tiled=True)
    key_blocks, order = tree_gather(key_rows[0], z, y)

    next_gain = lax.ppermute(gain, "section", back)
    chosen = permutation[0]
    first = lax.dynamic_index_in_dim(arrivals, chosen, 0, keepdims=False)
    sequences = [phase, jnp.where(phase == 0, phases + chosen, phase - 1)]
    bounds = [
        document_bounds(lax.dynamic_index_in_dim(lengths, s, 0, keepdims=False), context * tokens)
        for s in sequences
    ]
    is_last = (phase == phases - 1).astype(jnp.int32).reshape(1)
    info = jnp.concatenate([window_places(y), *bounds, is_last])

    mean = jnp.mean(stream * stream, axis=-1, keepdims=True)
    normed = (stream * lax.rsqrt(mean + EPSILON) * gain).astype(jnp.bfloat16)
    keys = projection(normed, order, key_blocks)
    keys, info, first = lax.optimization_barrier((keys, info, first))
    own = projection(normed, order, (), keys, value_weights, WHOLE)
    early, late = window_blocks(own, y)
    part = attention(early, info, 0, normed)
    produced, stream, normed = attention(late, info, 0, normed, part, stream, (first, next_gain))
    normed = lax.ppermute(normed, "section", onward)
    normed, stream = lax.optimization_barrier((normed, stream))
    stream = lax.ppermute(stream, "section", onward)
    own = projection(normed, order, key_blocks, None, value_weights)
    early, late = window_blocks(own, y)
    part = attention(early, info, 1, normed)
    (produced,) = attention(late, info, 1, normed, part, stream, None, produced)
    return produced[:, None]


def solution(mesh):
    placed = (
        P("section", "ctx", None),
        P(None, "ctx", None),
        P("section", None),
        P("section", "ctx", None),
        P("section", "ctx", None),
        P(),
        P(),
    )
    return jax.shard_map(
        shards,
        mesh=mesh,
        in_specs=placed,
        out_specs=P(None, "section", "ctx", None),
        check_vma=False,
    )
```

```python
import functools

import jax
import jax.numpy as jnp
from jax import lax
from jax.experimental import pallas as pl
from jax.experimental.pallas import tpu as pltpu
from jax.sharding import PartitionSpec as P

HEAD_SIZE = 128
QUERY_HEADS = 32
KEY_VALUE_HEADS = 4
HEAD_GROUPS = QUERY_HEADS // KEY_VALUE_HEADS
GROUP_WIDTH = HEAD_GROUPS * HEAD_SIZE
KV_WIDTH = KEY_VALUE_HEADS * HEAD_SIZE
W = 2
EPSILON = 1e-05
MASK_FLOOR = -1e30
SIDE = 4
VMEM = 28 << 20
WHOLE = 56 << 20
DOCUMENTS = 8
PLACES = 9
INFO = PLACES + W * (1 + DOCUMENTS) + 1
TOGETHER = 4
DEPTH = 256
SCALE = HEAD_SIZE ** (-0.5)
LOG2E = 1.4426950408889634


def moved(block, dz, dy):
    pairs = [
        (z * SIDE + y, ((z + dz) % SIDE) * SIDE + (y + dy) % SIDE)
        for z in range(SIDE)
        for y in range(SIDE)
    ]
    return lax.ppermute(block, "ctx", pairs)


def tree_gather(own, z, y):
    zp, yp, zm, ym = moved(own, 1, 0), moved(own, 0, 1), moved(own, -1, 0), moved(own, 0, -1)
    got = {(0, 0): own, (1, 0): zp, (0, 1): yp, (3, 0): zm, (0, 3): ym}
    got[0, 2], got[2, 0] = moved(own, 0, 2), moved(own, 2, 0)
    got[1, 1] = moved(zp, 0, 1)
    got[3, 3] = moved(zm, 0, -1)
    got[1, 3] = moved(ym, 1, 0)
    got[3, 1] = moved(yp, -1, 0)
    got[1, 2] = moved(got[0, 2], 1, 0)
    got[3, 2] = moved(got[0, 2], -1, 0)
    got[2, 1] = moved(got[2, 0], 0, 1)
    got[2, 3] = moved(got[2, 0], 0, -1)
    got[2, 2] = moved(got[1, 2], 1, 0)
    order = [((z - dz) % SIDE) * SIDE + (y - dy) % SIDE for dz, dy in got]
    return list(got.values()), jnp.stack(order)


def window_places(y):
    yl, yr, yf = (y + 3) % SIDE, (y + 1) % SIDE, (y + 2) % SIDE
    above = [SIDE + y - c for c in (yl, yr, yf)]
    near = [jnp.where(c < y, 0, 2 * SIDE) + y - c for c in (yl, yr, yf)]
    return jnp.stack([jnp.zeros_like(y), SIDE + 0 * y, 2 * SIDE + 0 * y, *above, *near])


def window_blocks(own, y):
    up1 = moved(own, 1, 0)
    up2 = moved(up1, 1, 0)
    above = [moved(up1, 0, 1), moved(up1, 0, -1), moved(up1, 0, 2)]
    to_right = jnp.where(y == SIDE - 1, up2, own)
    to_left = jnp.where(y == 0, own, up2)
    across = jnp.where(y < 2, own, up2)
    near = [moved(to_right, 0, 1), moved(to_left, 0, -1), moved(across, 0, 2)]
    return [own, up1, up2, *above], near


def fetched(blocks, into, sems, first=0):
    copies, row = [], 0
    for i, block in enumerate(blocks):
        height = block.shape[0]
        copies.append(pltpu.make_async_copy(block, into.at[pl.ds(row, height)], sems.at[first + i]))
        row += height
    for copy in copies:
        copy.start()
    return copies


def by_head(out, rows, which, beside):
    if not beside:
        out[...] = rows
        return
    for h in range(KEY_VALUE_HEADS):
        at = (2 * h + which) * HEAD_SIZE
        out[:, at : at + HEAD_SIZE] = rows[:, h * HEAD_SIZE : (h + 1) * HEAD_SIZE]


def projection_body(n_keys, with_keys, with_values, order, rows, *refs):
    key_blocks, refs = refs[:n_keys], refs[n_keys:]
    if with_keys:
        keys, refs = refs[0], refs[1:]
    if with_values:
        value_rows, refs = refs[0], refs[1:]
    out, refs = refs[0], list(refs[1:])
    sems = refs.pop()
    width = rows.shape[1]
    count = width // DEPTH
    if n_keys:
        held_keys = refs.pop(0)
        key_copies = fetched(key_blocks, held_keys, sems)
    if with_values:
        held_values = refs.pop(0)
        pieces = [value_rows.at[pl.ds(j * DEPTH, DEPTH)] for j in range(count)]
        value_copies = fetched(pieces, held_values, sems, n_keys)
    if n_keys:
        total = jnp.zeros((rows.shape[0], KV_WIDTH), jnp.float32)
        for j, copy in enumerate(key_copies):
            copy.wait()
            at = pl.ds(pl.multiple_of(order[j] * DEPTH, DEPTH), DEPTH)
            part = held_keys[j * DEPTH : (j + 1) * DEPTH]
            total = total + jnp.dot(rows[:, at], part, preferred_element_type=jnp.float32)
        by_head(out, total.astype(out.dtype), 0, with_values)
    if with_keys:
        by_head(out, keys[...], 0, True)
    if with_values:
        total = jnp.zeros((rows.shape[0], KV_WIDTH), jnp.float32)
        for j, copy in enumerate(value_copies):
            copy.wait()
            at = slice(j * DEPTH, (j + 1) * DEPTH)
            total = total + jnp.dot(rows[:, at], held_values[at], preferred_element_type=jnp.float32)
        by_head(out, total.astype(out.dtype), 1, True)


def projection(rows, order, key_blocks=(), keys=None, values=None, vmem=VMEM):
    tokens, width = rows.shape
    n_keys = len(key_blocks)
    in_vmem, in_hbm = pl.BlockSpec(memory_space=pltpu.VMEM), pl.BlockSpec(memory_space=pl.ANY)
    in_specs = [pl.BlockSpec(memory_space=pltpu.SMEM), in_vmem] + [in_hbm] * n_keys
    operands = [order, rows, *key_blocks]
    held = pltpu.VMEM((width, KV_WIDTH), jnp.bfloat16)
    scratch = [held] if n_keys else []
    n_copies, columns = n_keys, KV_WIDTH
    if keys is not None:
        in_specs, operands = in_specs + [in_vmem], operands + [keys]
    if values is not None:
        in_specs, operands = in_specs + [in_hbm], operands + [values]
        scratch, n_copies, columns = scratch + [held], n_copies + width // DEPTH, 2 * KV_WIDTH
    return pl.pallas_call(
        functools.partial(projection_body, n_keys, keys is not None, values is not None),
        in_specs=in_specs,
        out_specs=in_vmem,
        out_shape=jax.ShapeDtypeStruct((tokens, columns), jnp.bfloat16),
        scratch_shapes=[*scratch, pltpu.SemaphoreType.DMA((n_copies,))],
        compiler_params=pltpu.CompilerParams(vmem_limit_bytes=vmem),
        cost_estimate=pl.CostEstimate(
            flops=2 * tokens * width * KV_WIDTH * len(scratch),
            transcendentals=0,
            bytes_accessed=len(scratch) * width * KV_WIDTH * 2,
        ),
        name="projection",
    )(*operands)


def attention_body(n_blocks, stage, tick, info, q, *refs):
    blocks, refs = refs[:n_blocks], refs[n_blocks:]
    if stage == "first":
        out_mix, out_sum, out_high = refs
    elif stage == "last":
        x, mix, sums, highs, _, produced = refs
    else:
        x, mix, sums, highs, first, gain, produced, stream, normed, rows, squares = refs
    g = pl.program_id(0)
    tokens = q.shape[0]
    column = lax.broadcasted_iota(jnp.int32, (tokens, tokens), 1)
    row = lax.broadcasted_iota(jnp.int32, (tokens, tokens), 0)
    ends = PLACES + tick * (1 + DOCUMENTS)
    low = jnp.full((tokens, tokens), info[ends], jnp.int32)
    for j in range(1, 1 + DOCUMENTS):
        low = jnp.where(row >= info[ends + j], info[ends + j], low)
    bias = []
    for b in range(n_blocks):
        place = info[b if stage == "first" else PLACES - n_blocks + b]
        allowed = column - place * tokens >= low
        if stage == "first" and b == 0:
            allowed = allowed & (column <= row)
        bias.append(jnp.where(allowed, 0.0, MASK_FLOOR))
    bias = jnp.concatenate(bias, axis=1)
    bias = jnp.concatenate([bias] * TOGETHER, axis=0)
    k = jnp.concatenate([block[:, :HEAD_SIZE] for block in blocks], axis=0)
    v = jnp.concatenate([block[:, HEAD_SIZE:] for block in blocks], axis=0)
    v = jnp.concatenate([v, jnp.ones_like(v)], axis=1)
    squared = None
    for h in range(0, HEAD_GROUPS, TOGETHER):
        qs = [q[:, (h + j) * HEAD_SIZE : (h + j + 1) * HEAD_SIZE] for j in range(TOGETHER)]
        s = lax.dot_general(
            jnp.concatenate(qs, axis=0),
            k,
            (((1,), (1,)), ((), ())),
            preferred_element_type=jnp.float32,
        )
        s = s + bias
        here = slice(h * tokens, (h + TOGETHER) * tokens)
        high = jnp.max(s, axis=1, keepdims=True)
        high = jnp.broadcast_to(high, (high.shape[0], HEAD_SIZE))
        if stage != "first":
            before = highs[here]
            high = jnp.maximum(high, before)
        p = jnp.concatenate(
            [
                jnp.exp2((s[:, c : c + HEAD_SIZE] - high) * (SCALE * LOG2E))
                for c in range(0, s.shape[1], HEAD_SIZE)
            ],
            axis=1,
        ).astype(jnp.bfloat16)
        mixed = jnp.dot(p, v, preferred_element_type=jnp.float32)
        mixed, total = mixed[:, :HEAD_SIZE], mixed[:, HEAD_SIZE:]
        if stage == "first":
            out_mix[here], out_sum[here], out_high[here] = mixed, total, high
            continue
        kept = jnp.exp2((before - high) * (SCALE * LOG2E))
        out = (mixed + mix[here] * kept) / (total + sums[here] * kept)
        for j in range(TOGETHER):
            where = slice((h + j) * HEAD_SIZE, (h + j + 1) * HEAD_SIZE)
            new = x[:, where] + out[j * tokens : (j + 1) * tokens]
            produced[0, :, where] = new.astype(jnp.bfloat16)
            if stage != "last":
                new = jnp.where(info[INFO - 1] == 1, first[:, where].astype(jnp.float32), new)
                stream[:, where] = new
                at = pl.multiple_of(g * GROUP_WIDTH, GROUP_WIDTH) + (h + j) * HEAD_SIZE
                rows[:, pl.ds(at, HEAD_SIZE)] = new
                squared = new * new if squared is None else squared + new * new
    if stage != "onward":
        return
    squares[...] = jnp.where(g == 0, squared, squares[...] + squared)

    @pl.when(g == KEY_VALUE_HEADS - 1)
    def _():
        mean = jnp.sum(squares[...], axis=1, keepdims=True) * (1.0 / rows.shape[1])
        factor = lax.rsqrt(mean + EPSILON)
        for c in range(0, rows.shape[1], 128):
            at = slice(c, c + 128)
            normed[:, at] = (rows[:, at] * factor * gain[:, at]).astype(jnp.bfloat16)


def attention(blocks, info, tick, q, part=None, x=None, onward=None, produced=None):
    tokens, width = q.shape
    n_blocks = len(blocks)
    span = n_blocks * tokens
    stage = "first" if part is None else "last" if onward is None else "onward"
    whole = lambda g, *_: (0, 0)
    by_group = pl.BlockSpec((tokens, GROUP_WIDTH), lambda g, *_: (0, g))
    by_rows = pl.BlockSpec((HEAD_GROUPS * tokens, HEAD_SIZE), lambda g, *_: (g, 0))
    in_specs = [by_group]
    in_specs += [pl.BlockSpec((tokens, 2 * HEAD_SIZE), lambda g, *_: (0, g))] * n_blocks
    operands = [q, *blocks]
    scratch = []
    aliases = {}
    if stage == "first":
        out_specs = [by_rows] * 3
        out_shape = [jax.ShapeDtypeStruct((QUERY_HEADS * tokens, HEAD_SIZE), jnp.float32)] * 3
    else:
        in_specs += [by_group] + [by_rows] * 3
        operands += [x, *part]
        out_specs = [pl.BlockSpec((1, tokens, GROUP_WIDTH), lambda g, *_: (tick, 0, g))]
        out_shape = [jax.ShapeDtypeStruct((W, tokens, width), jnp.bfloat16)]
    if stage == "last":
        aliases = {1 + len(operands): 0}
        in_specs += [pl.BlockSpec(memory_space=pl.ANY)]
        operands += [produced]
    if stage == "onward":
        in_specs += [by_group, pl.BlockSpec((1, width), whole)]
        operands += [*onward]
        out_specs += [by_group, pl.BlockSpec((tokens, width), whole)]
        out_shape += [
            jax.ShapeDtypeStruct((tokens, width), jnp.float32),
            jax.ShapeDtypeStruct((tokens, width), jnp.bfloat16),
        ]
        scratch += [pltpu.VMEM((tokens, width), jnp.float32), pltpu.VMEM((tokens, HEAD_SIZE), jnp.float32)]
    return pl.pallas_call(
        functools.partial(attention_body, n_blocks, stage, tick),
        grid_spec=pltpu.PrefetchScalarGridSpec(
            num_scalar_prefetch=1,
            grid=(KEY_VALUE_HEADS,),
            in_specs=in_specs,
            out_specs=out_specs,
            scratch_shapes=scratch,
        ),
        out_shape=out_shape,
        input_output_aliases=aliases,
        compiler_params=pltpu.CompilerParams(vmem_limit_bytes=VMEM),
        cost_estimate=pl.CostEstimate(
            flops=4 * tokens * span * width,
            transcendentals=tokens * span * QUERY_HEADS,
            bytes_accessed=tokens * width * 12 + span * 2 * KV_WIDTH * 2,
        ),
        name="attention",
    )(info, *operands)


def document_bounds(lengths, own_first):
    count = lengths.shape[0]
    upto = jnp.arange(count + 1)[:, None] > jnp.arange(count)[None, :]
    return jnp.sum(jnp.where(upto, lengths[None, :], 0), axis=1) - own_first


def shards(carried, arrivals, gains, key_rows, value_rows, lengths, permutation):
    stream = carried[0]
    gain = gains[0:1]
    tokens = stream.shape[0]
    phases = lax.axis_size("section")
    phase = lax.axis_index("section")
    context = lax.axis_index("ctx")
    z, y = context // SIDE, context % SIDE
    onward = [(s, (s + 1) % phases) for s in range(phases)]
    back = [(t, s) for s, t in onward]

    value_weights = lax.all_gather(value_rows[0], "ctx", axis=0, tiled=True)
    key_blocks, order = tree_gather(key_rows[0], z, y)

    next_gain = lax.ppermute(gain, "section", back)
    chosen = permutation[0]
    first = lax.dynamic_index_in_dim(arrivals, chosen, 0, keepdims=False)
    sequences = [phase, jnp.where(phase == 0, phases + chosen, phase - 1)]
    bounds = [
        document_bounds(lax.dynamic_index_in_dim(lengths, s, 0, keepdims=False), context * tokens)
        for s in sequences
    ]
    is_last = (phase == phases - 1).astype(jnp.int32).reshape(1)
    info = jnp.concatenate([window_places(y), *bounds, is_last])

    mean = jnp.mean(stream * stream, axis=-1, keepdims=True)
    normed = (stream * lax.rsqrt(mean + EPSILON) * gain).astype(jnp.bfloat16)
    keys = projection(normed, order, key_blocks)
    keys, info, first = lax.optimization_barrier((keys, info, first))
    own = projection(normed, order, (), keys, value_weights, WHOLE)
    early, late = window_blocks(own, y)
    part = attention(early, info, 0, normed)
    produced, stream, normed = attention(late, info, 0, normed, part, stream, (first, next_gain))
    normed = lax.ppermute(normed, "section", onward)
    normed, stream = lax.optimization_barrier((normed, stream))
    stream = lax.ppermute(stream, "section", onward)
    own = projection(normed, order, key_blocks, None, value_weights)
    early, late = window_blocks(own, y)
    part = attention(early, info, 1, normed)
    (produced,) = attention(late, info, 1, normed, part, stream, None, produced)
    return produced[:, None]


def solution(mesh):
    placed = (
        P("section", "ctx", None),
        P(None, "ctx", None),
        P("section", None),
        P("section", "ctx", None),
        P("section", "ctx", None),
        P(),
        P(),
    )
    return jax.shard_map(
        shards,
        mesh=mesh,
        in_specs=placed,
        out_specs=P(None, "section", "ctx", None),
        check_vma=False,
    )
```

```python
import functools

import jax
import jax.numpy as jnp
from jax import lax
from jax.experimental import pallas as pl
from jax.experimental.pallas import tpu as pltpu
from jax.sharding import PartitionSpec as P

HEAD_SIZE = 128
QUERY_HEADS = 32
KEY_VALUE_HEADS = 4
HEAD_GROUPS = QUERY_HEADS // KEY_VALUE_HEADS
GROUP_WIDTH = HEAD_GROUPS * HEAD_SIZE
KV_WIDTH = KEY_VALUE_HEADS * HEAD_SIZE
W = 2
EPSILON = 1e-05
MASK_FLOOR = -1e30
SIDE = 4
VMEM = 28 << 20
WHOLE = 56 << 20
DOCUMENTS = 8
PLACES = 9
INFO = PLACES + W * (1 + DOCUMENTS) + 1
TOGETHER = 4
FIRST_TOGETHER = 2
DEPTH = 256
SCALE = HEAD_SIZE ** (-0.5)
LOG2E = 1.4426950408889634


def moved(block, dz, dy):
    pairs = [
        (z * SIDE + y, ((z + dz) % SIDE) * SIDE + (y + dy) % SIDE)
        for z in range(SIDE)
        for y in range(SIDE)
    ]
    return lax.ppermute(block, "ctx", pairs)


def tree_gather(own, z, y):
    zp, yp, zm, ym = moved(own, 1, 0), moved(own, 0, 1), moved(own, -1, 0), moved(own, 0, -1)
    got = {(0, 0): own, (1, 0): zp, (0, 1): yp, (3, 0): zm, (0, 3): ym}
    got[0, 2], got[2, 0] = moved(own, 0, 2), moved(own, 2, 0)
    got[1, 1] = moved(zp, 0, 1)
    got[3, 3] = moved(zm, 0, -1)
    got[1, 3] = moved(ym, 1, 0)
    got[3, 1] = moved(yp, -1, 0)
    got[1, 2] = moved(got[0, 2], 1, 0)
    got[3, 2] = moved(got[0, 2], -1, 0)
    got[2, 1] = moved(got[2, 0], 0, 1)
    got[2, 3] = moved(got[2, 0], 0, -1)
    got[2, 2] = moved(got[1, 2], 1, 0)
    order = [((z - dz) % SIDE) * SIDE + (y - dy) % SIDE for dz, dy in got]
    return list(got.values()), jnp.stack(order)


def window_places(y):
    yl, yr, yf = (y + 3) % SIDE, (y + 1) % SIDE, (y + 2) % SIDE
    above = [SIDE + y - c for c in (yl, yr, yf)]
    near = [jnp.where(c < y, 0, 2 * SIDE) + y - c for c in (yl, yr, yf)]
    return jnp.stack([jnp.zeros_like(y), SIDE + 0 * y, 2 * SIDE + 0 * y, *above, *near])


def window_blocks(own, y):
    up1 = moved(own, 1, 0)
    up2 = moved(up1, 1, 0)
    above = [moved(up1, 0, 1), moved(up1, 0, -1), moved(up1, 0, 2)]
    to_right = jnp.where(y == SIDE - 1, up2, own)
    to_left = jnp.where(y == 0, own, up2)
    across = jnp.where(y < 2, own, up2)
    near = [moved(to_right, 0, 1), moved(to_left, 0, -1), moved(across, 0, 2)]
    return [own, up1, up2, *above], near


def fetched(blocks, into, sems, first=0):
    copies, row = [], 0
    for i, block in enumerate(blocks):
        height = block.shape[0]
        copies.append(pltpu.make_async_copy(block, into.at[pl.ds(row, height)], sems.at[first + i]))
        row += height
    for copy in copies:
        copy.start()
    return copies


def by_head(out, rows, which, beside):
    if not beside:
        out[...] = rows
        return
    for h in range(KEY_VALUE_HEADS):
        at = (2 * h + which) * HEAD_SIZE
        out[:, at : at + HEAD_SIZE] = rows[:, h * HEAD_SIZE : (h + 1) * HEAD_SIZE]


def projection_body(n_keys, with_keys, with_values, order, rows, *refs):
    key_blocks, refs = refs[:n_keys], refs[n_keys:]
    if with_keys:
        keys, refs = refs[0], refs[1:]
    if with_values:
        value_rows, refs = refs[0], refs[1:]
    out, refs = refs[0], list(refs[1:])
    sems = refs.pop()
    width = rows.shape[1]
    count = width // DEPTH
    if n_keys:
        held_keys = refs.pop(0)
        key_copies = fetched(key_blocks, held_keys, sems)
    if with_values:
        held_values = refs.pop(0)
        pieces = [value_rows.at[pl.ds(j * DEPTH, DEPTH)] for j in range(count)]
        value_copies = fetched(pieces, held_values, sems, n_keys)
    if n_keys:
        total = jnp.zeros((rows.shape[0], KV_WIDTH), jnp.float32)
        for j, copy in enumerate(key_copies):
            copy.wait()
            at = pl.ds(pl.multiple_of(order[j] * DEPTH, DEPTH), DEPTH)
            part = held_keys[j * DEPTH : (j + 1) * DEPTH]
            total = total + jnp.dot(rows[:, at], part, preferred_element_type=jnp.float32)
        by_head(out, total.astype(out.dtype), 0, with_values)
    if with_keys:
        by_head(out, keys[...], 0, True)
    if with_values:
        total = jnp.zeros((rows.shape[0], KV_WIDTH), jnp.float32)
        for j, copy in enumerate(value_copies):
            copy.wait()
            at = slice(j * DEPTH, (j + 1) * DEPTH)
            total = total + jnp.dot(rows[:, at], held_values[at], preferred_element_type=jnp.float32)
        by_head(out, total.astype(out.dtype), 1, True)


def projection(rows, order, key_blocks=(), keys=None, values=None, vmem=VMEM):
    tokens, width = rows.shape
    n_keys = len(key_blocks)
    in_vmem, in_hbm = pl.BlockSpec(memory_space=pltpu.VMEM), pl.BlockSpec(memory_space=pl.ANY)
    in_specs = [pl.BlockSpec(memory_space=pltpu.SMEM), in_vmem] + [in_hbm] * n_keys
    operands = [order, rows, *key_blocks]
    held = pltpu.VMEM((width, KV_WIDTH), jnp.bfloat16)
    scratch = [held] if n_keys else []
    n_copies, columns = n_keys, KV_WIDTH
    if keys is not None:
        in_specs, operands = in_specs + [in_vmem], operands + [keys]
    if values is not None:
        in_specs, operands = in_specs + [in_hbm], operands + [values]
        scratch, n_copies, columns = scratch + [held], n_copies + width // DEPTH, 2 * KV_WIDTH
    return pl.pallas_call(
        functools.partial(projection_body, n_keys, keys is not None, values is not None),
        in_specs=in_specs,
        out_specs=in_vmem,
        out_shape=jax.ShapeDtypeStruct((tokens, columns), jnp.bfloat16),
        scratch_shapes=[*scratch, pltpu.SemaphoreType.DMA((n_copies,))],
        compiler_params=pltpu.CompilerParams(vmem_limit_bytes=vmem),
        cost_estimate=pl.CostEstimate(
            flops=2 * tokens * width * KV_WIDTH * len(scratch),
            transcendentals=0,
            bytes_accessed=len(scratch) * width * KV_WIDTH * 2,
        ),
        name="projection",
    )(*operands)


def attention_body(n_blocks, stage, tick, info, q, *refs):
    blocks, refs = refs[:n_blocks], refs[n_blocks:]
    if stage == "first":
        out_mix, out_sum, out_high = refs
    elif stage == "last":
        x, mix, sums, highs, _, produced = refs
    else:
        x, mix, sums, highs, first, gain, produced, stream, normed, rows, squares = refs
    together = FIRST_TOGETHER if stage == "first" else TOGETHER
    g = pl.program_id(0)
    tokens = q.shape[0]
    column = lax.broadcasted_iota(jnp.int32, (tokens, tokens), 1)
    row = lax.broadcasted_iota(jnp.int32, (tokens, tokens), 0)
    ends = PLACES + tick * (1 + DOCUMENTS)
    low = jnp.full((tokens, tokens), info[ends], jnp.int32)
    for j in range(1, 1 + DOCUMENTS):
        low = jnp.where(row >= info[ends + j], info[ends + j], low)
    bias = []
    for b in range(n_blocks):
        place = info[b if stage == "first" else PLACES - n_blocks + b]
        allowed = column - place * tokens >= low
        if stage == "first" and b == 0:
            allowed = allowed & (column <= row)
        bias.append(jnp.where(allowed, 0.0, MASK_FLOOR))
    bias = jnp.concatenate(bias, axis=1)
    bias = jnp.concatenate([bias] * together, axis=0)
    k = jnp.concatenate([block[:, :HEAD_SIZE] for block in blocks], axis=0)
    v = jnp.concatenate([block[:, HEAD_SIZE:] for block in blocks], axis=0)
    v = jnp.concatenate([v, jnp.ones_like(v)], axis=1)
    squared = None
    for h in range(0, HEAD_GROUPS, together):
        qs = [q[:, (h + j) * HEAD_SIZE : (h + j + 1) * HEAD_SIZE] for j in range(together)]
        s = lax.dot_general(
            jnp.concatenate(qs, axis=0),
            k,
            (((1,), (1,)), ((), ())),
            preferred_element_type=jnp.float32,
        )
        s = s + bias
        here = slice(h * tokens, (h + together) * tokens)
        high = jnp.max(s, axis=1, keepdims=True)
        high = jnp.broadcast_to(high, (high.shape[0], HEAD_SIZE))
        if stage != "first":
            before = highs[here]
            high = jnp.maximum(high, before)
        p = jnp.concatenate(
            [
                jnp.exp2((s[:, c : c + HEAD_SIZE] - high) * (SCALE * LOG2E))
                for c in range(0, s.shape[1], HEAD_SIZE)
            ],
            axis=1,
        ).astype(jnp.bfloat16)
        mixed = jnp.dot(p, v, preferred_element_type=jnp.float32)
        mixed, total = mixed[:, :HEAD_SIZE], mixed[:, HEAD_SIZE:]
        if stage == "first":
            out_mix[here], out_sum[here], out_high[here] = mixed, total, high
            continue
        kept = jnp.exp2((before - high) * (SCALE * LOG2E))
        out = (mixed + mix[here] * kept) / (total + sums[here] * kept)
        for j in range(together):
            where = slice((h + j) * HEAD_SIZE, (h + j + 1) * HEAD_SIZE)
            new = x[:, where] + out[j * tokens : (j + 1) * tokens]
            produced[0, :, where] = new.astype(jnp.bfloat16)
            if stage != "last":
                new = jnp.where(info[INFO - 1] == 1, first[:, where].astype(jnp.float32), new)
                stream[:, where] = new
                at = pl.multiple_of(g * GROUP_WIDTH, GROUP_WIDTH) + (h + j) * HEAD_SIZE
                rows[:, pl.ds(at, HEAD_SIZE)] = new
                squared = new * new if squared is None else squared + new * new
    if stage != "onward":
        return
    squares[...] = jnp.where(g == 0, squared, squares[...] + squared)

    @pl.when(g == KEY_VALUE_HEADS - 1)
    def _():
        mean = jnp.sum(squares[...], axis=1, keepdims=True) * (1.0 / rows.shape[1])
        factor = lax.rsqrt(mean + EPSILON)
        for c in range(0, rows.shape[1], 128):
            at = slice(c, c + 128)
            normed[:, at] = (rows[:, at] * factor * gain[:, at]).astype(jnp.bfloat16)


def attention(blocks, info, tick, q, part=None, x=None, onward=None, produced=None):
    tokens, width = q.shape
    n_blocks = len(blocks)
    span = n_blocks * tokens
    stage = "first" if part is None else "last" if onward is None else "onward"
    whole = lambda g, *_: (0, 0)
    by_group = pl.BlockSpec((tokens, GROUP_WIDTH), lambda g, *_: (0, g))
    by_rows = pl.BlockSpec((HEAD_GROUPS * tokens, HEAD_SIZE), lambda g, *_: (g, 0))
    in_specs = [by_group]
    in_specs += [pl.BlockSpec((tokens, 2 * HEAD_SIZE), lambda g, *_: (0, g))] * n_blocks
    operands = [q, *blocks]
    scratch = []
    aliases = {}
    if stage == "first":
        out_specs = [by_rows] * 3
        out_shape = [jax.ShapeDtypeStruct((QUERY_HEADS * tokens, HEAD_SIZE), jnp.float32)] * 3
    else:
        in_specs += [by_group] + [by_rows] * 3
        operands += [x, *part]
        out_specs = [pl.BlockSpec((1, tokens, GROUP_WIDTH), lambda g, *_: (tick, 0, g))]
        out_shape = [jax.ShapeDtypeStruct((W, tokens, width), jnp.bfloat16)]
    if stage == "last":
        aliases = {1 + len(operands): 0}
        in_specs += [pl.BlockSpec(memory_space=pl.ANY)]
        operands += [produced]
    if stage == "onward":
        in_specs += [by_group, pl.BlockSpec((1, width), whole)]
        operands += [*onward]
        out_specs += [by_group, pl.BlockSpec((tokens, width), whole)]
        out_shape += [
            jax.ShapeDtypeStruct((tokens, width), jnp.float32),
            jax.ShapeDtypeStruct((tokens, width), jnp.bfloat16),
        ]
        scratch += [pltpu.VMEM((tokens, width), jnp.float32), pltpu.VMEM((tokens, HEAD_SIZE), jnp.float32)]
    return pl.pallas_call(
        functools.partial(attention_body, n_blocks, stage, tick),
        grid_spec=pltpu.PrefetchScalarGridSpec(
            num_scalar_prefetch=1,
            grid=(KEY_VALUE_HEADS,),
            in_specs=in_specs,
            out_specs=out_specs,
            scratch_shapes=scratch,
        ),
        out_shape=out_shape,
        input_output_aliases=aliases,
        compiler_params=pltpu.CompilerParams(vmem_limit_bytes=VMEM),
        cost_estimate=pl.CostEstimate(
            flops=4 * tokens * span * width,
            transcendentals=tokens * span * QUERY_HEADS,
            bytes_accessed=tokens * width * 12 + span * 2 * KV_WIDTH * 2,
        ),
        name="attention",
    )(info, *operands)


def document_bounds(lengths, own_first):
    count = lengths.shape[0]
    upto = jnp.arange(count + 1)[:, None] > jnp.arange(count)[None, :]
    return jnp.sum(jnp.where(upto, lengths[None, :], 0), axis=1) - own_first


def shards(carried, arrivals, gains, key_rows, value_rows, lengths, permutation):
    stream = carried[0]
    gain = gains[0:1]
    tokens = stream.shape[0]
    phases = lax.axis_size("section")
    phase = lax.axis_index("section")
    context = lax.axis_index("ctx")
    z, y = context // SIDE, context % SIDE
    onward = [(s, (s + 1) % phases) for s in range(phases)]
    back = [(t, s) for s, t in onward]

    value_weights = lax.all_gather(value_rows[0], "ctx", axis=0, tiled=True)
    key_blocks, order = tree_gather(key_rows[0], z, y)

    next_gain = lax.ppermute(gain, "section", back)
    chosen = permutation[0]
    first = lax.dynamic_index_in_dim(arrivals, chosen, 0, keepdims=False)
    sequences = [phase, jnp.where(phase == 0, phases + chosen, phase - 1)]
    bounds = [
        document_bounds(lax.dynamic_index_in_dim(lengths, s, 0, keepdims=False), context * tokens)
        for s in sequences
    ]
    is_last = (phase == phases - 1).astype(jnp.int32).reshape(1)
    info = jnp.concatenate([window_places(y), *bounds, is_last])

    mean = jnp.mean(stream * stream, axis=-1, keepdims=True)
    normed = (stream * lax.rsqrt(mean + EPSILON) * gain).astype(jnp.bfloat16)
    keys = projection(normed, order, key_blocks)
    keys, info, first = lax.optimization_barrier((keys, info, first))
    own = projection(normed, order, (), keys, value_weights, WHOLE)
    early, late = window_blocks(own, y)
    part = attention(early, info, 0, normed)
    produced, stream, normed = attention(late, info, 0, normed, part, stream, (first, next_gain))
    normed = lax.ppermute(normed, "section", onward)
    normed, stream = lax.optimization_barrier((normed, stream))
    stream = lax.ppermute(stream, "section", onward)
    own = projection(normed, order, key_blocks, None, value_weights)
    early, late = window_blocks(own, y)
    part = attention(early, info, 1, normed)
    (produced,) = attention(late, info, 1, normed, part, stream, None, produced)
    return produced[:, None]


def solution(mesh):
    placed = (
        P("section", "ctx", None),
        P(None, "ctx", None),
        P("section", None),
        P("section", "ctx", None),
        P("section", "ctx", None),
        P(),
        P(),
    )
    return jax.shard_map(
        shards,
        mesh=mesh,
        in_specs=placed,
        out_specs=P(None, "section", "ctx", None),
        check_vma=False,
    )
```
